256 devices in a mesh: dp: 64 (over x, z, core), mp: 4 (over y).
Axes of the slice: x: 4, y: 4, z: 8, core: 2. Of those that a mesh axis runs over, the one named last changes fastest.
Arguments:
- query_rows: bfloat16 [16384, 2048], P('dp', 'mp'), may hold values from -6 to 6
- key_rows: bfloat16 [16384, 512], P('dp', 'mp'), may hold values from -6 to 6
- value_matrix: bfloat16 [16384, 512], P('dp', 'mp'), may hold values from -6 to 6
- out_weight: bfloat16 [2048, 5120], P('mp', 'dp'), may hold values from -0.125 to 0.125
- out_grad: bfloat16 [16384, 5120], P('dp', 'mp'), may hold values from -16 to 16
- doc_lengths: int32 [64, 8], P('dp'), may hold values from 1 to 249, as said below
Outputs:
- layer_out: bfloat16 [16384, 5120], P('dp', 'mp')
- query_grad: bfloat16 [16384, 2048], P('dp', 'mp')
- key_grad: bfloat16 [16384, 512], P('dp', 'mp')
- value_grad: bfloat16 [16384, 512], P('dp', 'mp')
- weight_grad: float32 [2048, 5120], P('mp', 'dp')
The draws below stay inside these ranges and needn't reach their ends.
Inputs may be any that keep to these rules, and one draw needn't show every extreme that they name: `doc_lengths`: each row holds 8 lengths of 1 or more that sum to 256.
All inputs are finite; a program needn't handle non-finite values.
Results may differ from the reference program's by a relative error of at most 0.014.
Values may be sent and summed in bfloat16 or wider, within the bound.
No kernel may reach another device: no remote copies, remote signals or barrier semaphores. Data moves between devices by JAX's collectives and lax.ppermute only.
A program may use at most 64 MiB of HBM per device.

```python
import jax
import jax.numpy as jnp
from jax import lax

D = 5120
HQ = 16
KEY_VALUE_HEADS = 4
HEAD_WIDTH = 128
SEQ_DEV = 8
TOK_DEV = 256
TOKEN_TOTAL = 16384
N_DP = 64
N_MP = 4


def drawn_pair(key):
    base = jax.random.fold_in(key, 4021)
    query_key, key_random_seed = jax.random.split(base, 2)
    queries = jax.random.truncated_normal(query_key, -6.0, 6.0, (TOKEN_TOTAL, HQ * HEAD_WIDTH), jnp.float32)
    sampled_keys = jax.random.truncated_normal(key_random_seed, -6.0, 6.0, (TOKEN_TOTAL, KEY_VALUE_HEADS * HEAD_WIDTH), jnp.float32)
    return (queries, sampled_keys)


def draw_query_rows(key, part):
    return drawn_pair(key)[0].astype(jnp.bfloat16)


def draw_key_rows(key, part):
    return drawn_pair(key)[1].astype(jnp.bfloat16)


def draw_doc_lengths(key, part):
    base = jax.random.fold_in(key, 977)
    random_key, shift_key = jax.random.split(base)
    positions = jnp.arange(1, TOK_DEV, dtype=jnp.int32)
    shifts = jax.random.randint(shift_key, (N_DP, 1), 0, TOK_DEV, dtype=jnp.int32)
    device_rows = jnp.arange(N_DP, dtype=jnp.int32)[:, None]
    shifts = jnp.where(device_rows == 0, TOK_DEV - SEQ_DEV + 1, shifts)
    random_part = jax.random.randint(random_key, (N_DP, TOK_DEV - 1), 0, 4096, dtype=jnp.int32)
    scores = (random_part + 4096 * (positions[None, :] >= shifts).astype(jnp.int32)) * TOK_DEV + positions[None, :]
    picked = lax.top_k(scores, SEQ_DEV - 1)[1].astype(jnp.int32)
    cut_points = jnp.sort(picked + 1, axis=1)
    bounds = jnp.concatenate([jnp.zeros((N_DP, 1), jnp.int32), cut_points, jnp.full((N_DP, 1), TOK_DEV, jnp.int32)], axis=1)
    return jnp.diff(bounds, axis=1).astype(jnp.int32)


def raised(array, stream_key, source, target, parts, factor):
    def block_of(dim):
        return (jnp.arange(array.shape[dim]) // (array.shape[dim] // parts)).reshape((-1,) + (1,) * (array.ndim - 1 - dim))

    one_side = jax.random.permutation(stream_key, parts)[block_of(target)]
    other_side = (block_of(target) + parts // 2) % parts
    return jnp.where((block_of(source) == one_side) | (block_of(source) == other_side), factor * array, array)


def shard_levels(rng, extent, cuts, least, largest):
    gain = 1.0
    for axis_at, blocks in cuts:
        steps = jax.random.uniform(jax.random.fold_in(jax.random.fold_in(rng, 6), axis_at), (blocks,), jnp.float32, least / len(cuts), largest / len(cuts))
        gain = gain * jnp.repeat(jnp.exp(steps), extent[axis_at] // blocks).reshape((-1,) + (1,) * (len(extent) - 1 - axis_at))
    return gain


def normal_values(key, dims, spread, reach, shards=(), kind=jnp.bfloat16):
    drawn = spread * jax.random.normal(key, dims, jnp.float32)
    if shards:
        drawn = drawn * shard_levels(key, dims, shards, -0.22, 0.18)
    return jnp.clip(drawn, -reach, reach).astype(kind)


def gaussian_with(stream_key, extent, deviation, bound, cuts, heavy, kind=jnp.bfloat16):
    entries = deviation * jax.random.normal(stream_key, extent, jnp.float32)
    if cuts:
        entries = entries * shard_levels(stream_key, extent, cuts, -0.22, 0.18)
    return jnp.clip(raised(entries, jax.random.fold_in(stream_key, 3), *heavy), -bound, bound).astype(kind)


def setup_inputs(seed: int = 0) -> dict:
    streams_of = jax.random.split(jax.random.key(seed), 7)
    return {
        "query_rows": draw_query_rows(jax.random.fold_in(streams_of[6], 71), 0),
        "key_rows": draw_key_rows(jax.random.fold_in(streams_of[6], 71), 0),
        "value_matrix": normal_values(streams_of[2], (TOKEN_TOTAL, KEY_VALUE_HEADS * HEAD_WIDTH), 1.0, 6.0, ((0, 64), (1, 4))),
        "out_weight": normal_values(streams_of[3], (HQ * HEAD_WIDTH, D), (HQ * HEAD_WIDTH) ** -0.5, 0.125, ((0, 4), (1, 64))),
        "out_grad": gaussian_with(streams_of[4], (TOKEN_TOTAL, D), 1.0, 16.0, ((0, 64), (1, 4)), (0, 1, 64, 4.0)),
        "doc_lengths": draw_doc_lengths(jax.random.fold_in(streams_of[6], 71), 0),
    }


def local_segments(lengths, row_count):
    segment_ends = jnp.cumsum(lengths)
    positions = jnp.arange(row_count, dtype=jnp.int32)
    return jnp.sum((positions[:, None] >= segment_ends[None, :]).astype(jnp.int32), axis=1)


def split_heads(matrix):
    row_count = matrix.shape[0]
    return matrix.astype(jnp.float32).reshape(row_count, matrix.shape[1] // HEAD_WIDTH, HEAD_WIDTH).transpose(1, 0, 2)


def join_heads(tensor):
    return tensor.transpose(1, 0, 2).reshape(tensor.shape[1], tensor.shape[0] * HEAD_WIDTH)


def device_attention(queries_in, keys_in, values_in, upstream, segment):
    row_count = queries_in.shape[0]
    queries = split_heads(queries_in)
    kv_count = keys_in.shape[1] // HEAD_WIDTH
    group_size = queries.shape[0] // kv_count
    key_heads = jnp.repeat(split_heads(keys_in), group_size, axis=0)
    value_heads = jnp.repeat(split_heads(values_in), group_size, axis=0)
    upstreams = split_heads(upstream)
    softmax_scale = HEAD_WIDTH ** -0.5
    positions = jnp.arange(row_count, dtype=jnp.int32)
    allowed = (segment[:, None] == segment[None, :]) & (positions[:, None] >= positions[None, :])
    logits = jnp.einsum("hid,hjd->hij", queries, key_heads) * softmax_scale
    logits = jnp.where(allowed[None], logits, -jnp.inf)
    row_max = jnp.max(logits, axis=-1, keepdims=True)
    exp_terms = jnp.exp(logits - row_max)
    probability = exp_terms / jnp.sum(exp_terms, axis=-1, keepdims=True)
    weights = probability.astype(jnp.bfloat16).astype(jnp.float32)
    attended = jnp.einsum("hij,hjd->hid", weights, value_heads).astype(jnp.bfloat16)
    prob_grad = jnp.einsum("hid,hjd->hij", upstreams, value_heads)
    row_delta = jnp.sum(probability * prob_grad, axis=-1, keepdims=True)
    score_grad = (probability * (prob_grad - row_delta) * softmax_scale).astype(jnp.bfloat16).astype(jnp.float32)
    query_grad = jnp.einsum("hij,hjd->hid", score_grad, key_heads).astype(jnp.bfloat16)
    key_full = jnp.einsum("hij,hid->hjd", score_grad, queries)
    value_full = jnp.einsum("hij,hid->hjd", weights, upstreams)
    key_grad = key_full.reshape(kv_count, group_size, row_count, HEAD_WIDTH).sum(axis=1).astype(jnp.bfloat16)
    value_grad = value_full.reshape(kv_count, group_size, row_count, HEAD_WIDTH).sum(axis=1).astype(jnp.bfloat16)
    return join_heads(attended), join_heads(query_grad), join_heads(key_grad), join_heads(value_grad)


def reference(query_rows, key_rows, value_matrix, out_weight, out_grad, doc_lengths):
    attn_grad = jnp.dot(out_grad, out_weight.T, preferred_element_type=jnp.float32).astype(jnp.bfloat16)

    def per_device(pieces):
        queries_in, keys_in, values_in, upstream, lengths = pieces
        segment = local_segments(lengths, TOK_DEV)
        return device_attention(queries_in, keys_in, values_in, upstream, segment)

    stacked = (query_rows.reshape(N_DP, TOK_DEV, -1), key_rows.reshape(N_DP, TOK_DEV, -1),
               value_matrix.reshape(N_DP, TOK_DEV, -1), attn_grad.reshape(N_DP, TOK_DEV, -1), doc_lengths)
    attended, query_grad, key_grad, value_grad = lax.map(per_device, stacked)
    attended = attended.reshape(TOKEN_TOTAL, -1)
    query_grad = query_grad.reshape(TOKEN_TOTAL, -1)
    key_grad = key_grad.reshape(TOKEN_TOTAL, -1)
    value_grad = value_grad.reshape(TOKEN_TOTAL, -1)
    group_width = HQ * HEAD_WIDTH // N_MP
    total = jnp.zeros((TOKEN_TOTAL, D), jnp.float32)
    for group_index in range(N_MP):
        low_edge = group_index * group_width
        partial_sum = jnp.dot(attended[:, low_edge:low_edge + group_width], out_weight[low_edge:low_edge + group_width],
                              preferred_element_type=jnp.float32).astype(jnp.bfloat16)
        total = total + lax.optimization_barrier(partial_sum).astype(jnp.float32)
    layer_out = total.astype(jnp.bfloat16)
    weight_grad = jnp.dot(attended.T, out_grad, preferred_element_type=jnp.float32)
    return (layer_out, query_grad, key_grad, value_grad, weight_grad)
```

```python
import functools

import jax
import jax.numpy as jnp
from jax import lax
from jax.experimental import pallas as pl
from jax.experimental.pallas import tpu as pltpu
from jax.sharding import PartitionSpec as P

NX, NZ, NC, NY = 4, 8, 2, 4
HEAD = 128
TOK = 256
HEADS = 4
GROUP = HEADS * HEAD
COLS = 1280
SHARD = 80
FIRST = 32
REST = SHARD - FIRST
AXES = ("dp", "mp")
BF, F32 = jnp.bfloat16, jnp.float32
SCALE = HEAD ** -0.5


def route(target):
    pairs = []
    for x in range(NX):
        for z in range(NZ):
            for c in range(NC):
                for y in range(NY):
                    tx, tz, tc, ty = target(x, z, c, y)
                    src = ((x * NZ + z) * NC + c) * NY + y
                    pairs.append((src, ((tx * NZ + tz) * NC + tc) * NY + ty))
    return pairs


SWAP = route(lambda x, z, c, y: (x, z, 1 - c, y))
TO_PLANE = [route(lambda x, z, c, y, k=k: ((2 * (y % 2) + c + k) % 4, z, y // 2, x)) for k in range(4)]
TO_OWNER = [
    route(lambda x, z, c, y, k=k: (y, z, (x + k) % 4 % 2, 2 * c + (x + k) % 4 // 2)) for k in range(4)
]
HEADS_OUT = [route(lambda x, z, c, y, k=k: (x, z, y // 2, (2 * (y % 2) + c + k) % 4)) for k in range(4)]
HEADS_BACK = [
    route(lambda x, z, c, y, k=k: (x, z, (y + k) % 4 % 2, 2 * c + (y + k) % 4 // 2)) for k in range(4)
]
Z_GROUPS = [[(x * NZ + z) * NC + c for z in range(NZ)] for x in range(NX) for c in range(NC)]


def send(value, pairs):
    return lax.ppermute(value, AXES, pairs)


def over_z(blocks):
    return lax.all_to_all(blocks, "dp", 0, 0, axis_index_groups=Z_GROUPS, tiled=True)


def dot(a, b, dims):
    return lax.dot_general(a, b, (dims, ((), ())), preferred_element_type=F32)


def call(body, outs, scratch=(), flops=0, moved=0, prefetch=1, name=None):
    def run(scalars, *operands):
        vmem = pl.BlockSpec(memory_space=pltpu.VMEM)
        return pl.pallas_call(
            body,
            out_shape=outs,
            in_specs=[pl.BlockSpec(memory_space=pltpu.SMEM)] + [vmem] * len(operands),
            out_specs=jax.tree.map(lambda _: vmem, outs),
            scratch_shapes=list(scratch),
            compiler_params=pltpu.CompilerParams(vmem_limit_bytes=40 << 20),
            cost_estimate=pl.CostEstimate(flops=flops, bytes_accessed=moved, transcendentals=0),
            name=name,
        )(scalars, *operands)

    return run


def shape(*dims, dtype=BF):
    return jax.ShapeDtypeStruct(dims, dtype)


def forward_body(lengths, q_ref, k_ref, v_ref, att_ref, prob_ref):
    rows = lax.broadcasted_iota(jnp.int32, (TOK, TOK), 0)
    cols = lax.broadcasted_iota(jnp.int32, (TOK, TOK), 1)
    row_at = lax.broadcasted_iota(jnp.int32, (TOK, 1), 0)
    col_at = lax.broadcasted_iota(jnp.int32, (1, TOK), 1)
    row_seg = jnp.zeros((TOK, 1), jnp.int32)
    col_seg = jnp.zeros((1, TOK), jnp.int32)
    end = jnp.int32(0)
    for i in range(8):
        end = end + lengths[i]
        row_seg = row_seg + (row_at >= end).astype(jnp.int32)
        col_seg = col_seg + (col_at >= end).astype(jnp.int32)
    allowed = (row_seg == col_seg) & (rows >= cols)
    for h in range(HEADS):
        at = slice(h * HEAD, (h + 1) * HEAD)
        logits = dot(q_ref[:, at], k_ref[...], ((1,), (1,))) * SCALE
        logits = jnp.where(allowed, logits, -jnp.inf)
        terms = jnp.exp(logits - jnp.max(logits, axis=-1, keepdims=True))
        prob = terms / jnp.sum(terms, axis=-1, keepdims=True)
        prob_ref[h] = prob
        att_ref[:, at] = dot(prob.astype(BF), v_ref[...], ((1,), (0,))).astype(BF)


def backward_body(_, a0, a1, a2, a3, q_ref, k_ref, v_ref, prob_ref, dq_ref, dk_ref, dv_ref):
    key_sum = jnp.zeros((TOK, HEAD), F32)
    value_sum = jnp.zeros((TOK, HEAD), F32)
    for h in range(HEADS):
        at = slice(h * HEAD, (h + 1) * HEAD)
        up = (
            (a0[:, at].astype(F32) + a1[:, at].astype(F32))
            + (a2[:, at].astype(F32) + a3[:, at].astype(F32))
        ).astype(BF)
        prob = prob_ref[h]
        prob_grad = dot(up, v_ref[...], ((1,), (1,)))
        delta = jnp.sum(prob * prob_grad, axis=-1, keepdims=True)
        score = (prob * (prob_grad - delta) * SCALE).astype(BF)
        dq_ref[:, at] = dot(score, k_ref[...], ((1,), (0,))).astype(BF)
        key_sum = key_sum + dot(score, q_ref[:, at], ((0,), (0,)))
        value_sum = value_sum + dot(prob.astype(BF), up, ((0,), (0,)))
    dk_ref[...] = key_sum.astype(BF)
    dv_ref[...] = value_sum.astype(BF)


def weight_grad_body(place, own, other, r0, r1, r2, r3, first_ref, b0, b1, b2, b3, att_ref, og, total):
    x, c, y = place[0], place[1], place[2]
    og[pl.ds(pl.multiple_of(c * TOK, TOK), TOK), :] = own[...]
    og[pl.ds(pl.multiple_of((1 - c) * TOK, TOK), TOK), :] = other[...]
    for k, ref in enumerate((r0, r1, r2, r3)):
        j = (y + 4 - k) % 4
        att_ref[
            pl.ds(pl.multiple_of((j % 2) * TOK, TOK), TOK),
            pl.ds(pl.multiple_of((j // 2) * GROUP, GROUP), GROUP),
        ] = ref[...]
    for i in range(COLS // 256):
        total[i * 256 : (i + 1) * 256, :] = dot(
            og[:, i * 256 : (i + 1) * 256], att_ref[...], ((0,), (0,))
        ).astype(BF)
    for z in range(NZ):
        for j in range(4):
            first_ref[z, j * FIRST : (j + 1) * FIRST, :] = total[
                z * 160 + (j % 2) * SHARD : z * 160 + (j % 2) * SHARD + FIRST,
                (j // 2) * GROUP : (j // 2 + 1) * GROUP,
            ]
    for k, ref in enumerate((b0, b1, b2, b3)):
        j = (x + k) % 4
        for z in range(NZ):
            ref[z] = total[
                pl.ds(pl.multiple_of(z * 160 + (j % 2) * SHARD + FIRST, 16), REST),
                pl.ds(pl.multiple_of((j // 2) * GROUP, GROUP), GROUP),
            ]


def attn_grad_body(place, own, other, first, w0, w1, w2, w3, g0, g1, g2, g3, wt_ref, og):
    x, c, y = place[0], place[1], place[2]
    og[pl.ds(pl.multiple_of(c * TOK, TOK), TOK), :] = own[...]
    og[pl.ds(pl.multiple_of((1 - c) * TOK, TOK), TOK), :] = other[...]
    for k, ref in enumerate((w0, w1, w2, w3)):
        j = (x + 4 - k) % 4
        lanes = pl.ds(pl.multiple_of((j // 2) * GROUP, GROUP), GROUP)
        for z in range(NZ):
            base = z * 160 + (j % 2) * SHARD
            wt_ref[pl.ds(pl.multiple_of(base, 16), FIRST), lanes] = first[z, k * FIRST : (k + 1) * FIRST, :]
            wt_ref[pl.ds(pl.multiple_of(base + FIRST, 16), REST), lanes] = ref[z]
    for k, ref in enumerate((g0, g1, g2, g3)):
        m = (y + k) % 4
        ref[...] = dot(
            og[pl.ds(pl.multiple_of((m % 2) * TOK, TOK), TOK), :],
            wt_ref[:, pl.ds(pl.multiple_of((m // 2) * GROUP, GROUP), GROUP)],
            ((1,), (0,)),
        ).astype(BF)


def layer_out_body(place, att, wt, mine_ref, theirs_ref):
    c = place[1]
    mine_ref[...] = dot(att[pl.ds(pl.multiple_of(c * TOK, TOK), TOK), :], wt[...], ((1,), (1,)))
    theirs_ref[...] = dot(
        att[pl.ds(pl.multiple_of((1 - c) * TOK, TOK), TOK), :], wt[...], ((1,), (1,))
    ).astype(BF)


def sum_four_body(_, b0, b1, b2, b3, out):
    for z in range(NZ):
        out[z] = (
            (b0[z].astype(F32) + b1[z].astype(F32)) + (b2[z].astype(F32) + b3[z].astype(F32))
        ).astype(BF)


def sum_z_body(place, blocks, o0, o1, o2, o3):
    x = place[0]
    for k, ref in enumerate((o0, o1, o2, o3)):
        j = (x + k) % 4
        at = pl.ds(pl.multiple_of(j * FIRST, FIRST), FIRST)
        total = blocks[0, at, :].astype(F32)
        for z in range(1, NZ):
            total = total + blocks[z, at, :].astype(F32)
        ref[...] = total.astype(BF)


def finish_body(_, o0, o1, o2, o3, blocks, out):
    out[:FIRST, :] = (o0[...].astype(F32) + o1[...].astype(F32)) + (
        o2[...].astype(F32) + o3[...].astype(F32)
    )
    total = blocks[0].astype(F32)
    for z in range(1, NZ):
        total = total + blocks[z].astype(F32)
    out[FIRST:, :] = total


def per_device(query_rows, key_rows, value_matrix, out_weight, out_grad, doc_lengths):
    dp, y = lax.axis_index("dp"), lax.axis_index("mp")
    place = jnp.stack([dp // (NZ * NC), dp % NC, y]).astype(jnp.int32)
    wt = out_weight.T
    first_xy = [send(wt[:FIRST], pairs) for pairs in TO_PLANE]
    rest_z = over_z(jnp.broadcast_to(wt[FIRST:][None], (NZ, REST, GROUP)))
    other_grad = send(out_grad, SWAP)

    attended, prob = call(
        forward_body,
        (shape(TOK, GROUP), shape(HEADS, TOK, TOK, dtype=F32)),
        flops=4 * 4 * TOK * TOK * HEAD,
        moved=2 << 20,
        name="attention_forward",
    )(doc_lengths[0], query_rows, key_rows, value_matrix)
    heads = [send(attended, pairs) for pairs in HEADS_OUT]

    first_w = over_z(jnp.broadcast_to(jnp.concatenate(first_xy, axis=0)[None], (NZ, 4 * FIRST, GROUP)))
    rest_w = [send(rest_z, pairs) for pairs in TO_PLANE]

    big = 2 * 2 * TOK * COLS * 2 * GROUP
    grads = call(
        weight_grad_body,
        (shape(NZ, 4 * FIRST, GROUP),)
        + (shape(NZ, REST, GROUP),) * 4
        + (shape(2 * TOK, 2 * GROUP),),
        scratch=(pltpu.VMEM((2 * TOK, COLS), BF), pltpu.VMEM((COLS, 2 * GROUP), BF)),
        flops=big,
        moved=8 << 20,
        name="weight_grad",
    )(place, out_grad, other_grad, *heads)
    first_part, rest_parts, attended_two = grads[0], grads[1:5], grads[5]

    *partials, wt_two = call(
        attn_grad_body,
        (shape(TOK, GROUP),) * 4 + (shape(COLS, 2 * GROUP),),
        scratch=(pltpu.VMEM((2 * TOK, COLS), BF),),
        flops=big,
        moved=8 << 20,
        name="attn_grad",
    )(place, out_grad, other_grad, first_w, *rest_w)
    upstream = [send(partial, pairs) for partial, pairs in zip(partials, HEADS_BACK)]

    mine, theirs = call(
        layer_out_body,
        (shape(TOK, COLS, dtype=F32), shape(TOK, COLS)),
        flops=big,
        moved=6 << 20,
        name="layer_out",
    )(place, attended_two, wt_two)
    layer_out = (mine + send(theirs, SWAP).astype(F32)).astype(BF)

    rest_xy = [send(part, pairs) for part, pairs in zip(rest_parts, TO_OWNER)]
    first_sum = over_z(first_part)
    rest_sum = call(sum_four_body, shape(NZ, REST, GROUP), moved=2 << 20, name="sum_four")(
        place, *rest_xy
    )
    rest_sum = over_z(rest_sum)
    pieces = call(sum_z_body, (shape(FIRST, GROUP),) * 4, moved=1 << 20, name="sum_z")(place, first_sum)
    pieces = [send(piece, pairs) for piece, pairs in zip(pieces, TO_OWNER)]
    weight_grad = call(finish_body, shape(SHARD, GROUP, dtype=F32), moved=1 << 20, name="finish")(
        place, *pieces, rest_sum
    )

    query_grad, key_grad, value_grad = call(
        backward_body,
        (shape(TOK, GROUP), shape(TOK, HEAD), shape(TOK, HEAD)),
        flops=5 * 4 * 2 * TOK * TOK * HEAD,
        moved=3 << 20,
        name="attention_backward",
    )(place, *upstream, query_rows, key_rows, value_matrix, prob)
    return (layer_out, query_grad, key_grad, value_grad, weight_grad.T)


def solution(mesh):
    placed = (
        P("dp", "mp"),
        P("dp", "mp"),
        P("dp", "mp"),
        P("mp", "dp"),
        P("dp", "mp"),
        P("dp", None),
    )
    return jax.shard_map(
        per_device,
        mesh=mesh,
        in_specs=placed,
        out_specs=(P("dp", "mp"), P("dp", "mp"), P("dp", "mp"), P("dp", "mp"), P("mp", "dp")),
        check_vma=False,
    )
```

```python
import jax
import jax.numpy as jnp
from jax import lax
from jax.experimental import pallas as pl
from jax.experimental.pallas import tpu as pltpu
from jax.sharding import PartitionSpec as P


NX, NZ, NC, NY = 4, 8, 2, 4
HEAD = 128
TOK = 256
HEADS = 4
GROUP = HEADS * HEAD
COLS = 1280
SHARD = 80
FIRST = 48
REST = SHARD - FIRST
AXES = ("dp", "mp")
BF, F32 = jnp.bfloat16, jnp.float32
SCALE = HEAD ** -0.5


def route(target):
    pairs = []
    for x in range(NX):
        for z in range(NZ):
            for c in range(NC):
                for y in range(NY):
                    tx, tz, tc, ty = target(x, z, c, y)
                    src = ((x * NZ + z) * NC + c) * NY + y
                    pairs.append((src, ((tx * NZ + tz) * NC + tc) * NY + ty))
    return pairs


SWAP = route(lambda x, z, c, y: (x, z, 1 - c, y))
TO_PLANE = route(lambda x, z, c, y: (2 * (y % 2) + c, z, y // 2, x))
TO_OWNER = route(lambda x, z, c, y: (y, z, x % 2, 2 * c + x // 2))
HEADS_OUT = [route(lambda x, z, c, y, k=k: (x, z, y // 2, (2 * (y % 2) + c + k) % 4)) for k in range(4)]
HEADS_BACK = [
    route(lambda x, z, c, y, k=k: (x, z, (y + k) % 4 % 2, 2 * c + (y + k) % 4 // 2)) for k in range(4)
]
Z_GROUPS = [[(x * NZ + z) * NC + c for z in range(NZ)] for x in range(NX) for c in range(NC)]
X_GROUPS = [[(x * NZ + z) * NC + c for x in range(NX)] for z in range(NZ) for c in range(NC)]


def send(value, pairs):
    return lax.ppermute(value, AXES, pairs)


def exchange(blocks, groups):
    return lax.all_to_all(blocks, "dp", 0, 0, axis_index_groups=groups, tiled=True)


def gather(block, groups):
    return lax.all_gather(block, "dp", axis_index_groups=groups, tiled=True)


def scatter(blocks, groups):
    return lax.psum_scatter(blocks, "dp", axis_index_groups=groups, tiled=True)


def to_all(block, groups):
    return exchange(jnp.broadcast_to(block[None], (len(groups[0]), *block.shape)), groups)


def dot(a, b, dims):
    return lax.dot_general(a, b, (dims, ((), ())), preferred_element_type=F32)


def call(body, outs, scratch=(), flops=0, moved=0):
    def run(scalars, *operands):
        vmem = pl.BlockSpec(memory_space=pltpu.VMEM)
        return pl.pallas_call(
            body,
            out_shape=outs,
            in_specs=[pl.BlockSpec(memory_space=pltpu.SMEM)] + [vmem] * len(operands),
            out_specs=jax.tree.map(lambda _: vmem, outs),
            scratch_shapes=list(scratch),
            compiler_params=pltpu.CompilerParams(vmem_limit_bytes=40 << 20),
            cost_estimate=pl.CostEstimate(flops=flops, bytes_accessed=moved, transcendentals=0),
        )(scalars, *operands)

    return run


def shape(*dims, dtype=BF):
    return jax.ShapeDtypeStruct(dims, dtype)


def forward_body(lengths, q_ref, k_ref, v_ref, att_ref, prob_ref):
    rows = lax.broadcasted_iota(jnp.int32, (TOK, TOK), 0)
    cols = lax.broadcasted_iota(jnp.int32, (TOK, TOK), 1)
    row_at = lax.broadcasted_iota(jnp.int32, (TOK, 1), 0)
    col_at = lax.broadcasted_iota(jnp.int32, (1, TOK), 1)
    row_seg = jnp.zeros((TOK, 1), jnp.int32)
    col_seg = jnp.zeros((1, TOK), jnp.int32)
    end = jnp.int32(0)
    for i in range(8):
        end = end + lengths[i]
        row_seg = row_seg + (row_at >= end).astype(jnp.int32)
        col_seg = col_seg + (col_at >= end).astype(jnp.int32)
    allowed = (row_seg == col_seg) & (rows >= cols)
    for h in range(HEADS):
        at = slice(h * HEAD, (h + 1) * HEAD)
        logits = dot(q_ref[:, at], k_ref[...], ((1,), (1,))) * SCALE
        logits = jnp.where(allowed, logits, -jnp.inf)
        terms = jnp.exp(logits - jnp.max(logits, axis=-1, keepdims=True))
        prob = terms / jnp.sum(terms, axis=-1, keepdims=True)
        prob_ref[h] = prob
        att_ref[:, at] = dot(prob.astype(BF), v_ref[...], ((1,), (0,))).astype(BF)


def backward_body(_, a0, a1, a2, a3, q_ref, k_ref, v_ref, prob_ref, dq_ref, dk_ref, dv_ref):
    key_sum = jnp.zeros((TOK, HEAD), F32)
    value_sum = jnp.zeros((TOK, HEAD), F32)
    for h in range(HEADS):
        at = slice(h * HEAD, (h + 1) * HEAD)
        up = (
            (a0[:, at].astype(F32) + a1[:, at].astype(F32))
            + (a2[:, at].astype(F32) + a3[:, at].astype(F32))
        ).astype(BF)
        prob = prob_ref[h]
        prob_grad = dot(up, v_ref[...], ((1,), (1,)))
        delta = jnp.sum(prob * prob_grad, axis=-1, keepdims=True)
        score = (prob * (prob_grad - delta) * SCALE).astype(BF)
        dq_ref[:, at] = dot(score, k_ref[...], ((1,), (0,))).astype(BF)
        key_sum = key_sum + dot(score, q_ref[:, at], ((0,), (0,)))
        value_sum = value_sum + dot(prob.astype(BF), up, ((0,), (0,)))
    dk_ref[...] = key_sum.astype(BF)
    dv_ref[...] = value_sum.astype(BF)


def weight_grad_body(place, own, other, r0, r1, r2, r3, first_ref, rest_ref, att_ref, og, total):
    c, y = place[0], place[1]
    og[pl.ds(pl.multiple_of(c * TOK, TOK), TOK), :] = own[...]
    og[pl.ds(pl.multiple_of((1 - c) * TOK, TOK), TOK), :] = other[...]
    for k, ref in enumerate((r0, r1, r2, r3)):
        j = (y + 4 - k) % 4
        att_ref[
            pl.ds(pl.multiple_of((j % 2) * TOK, TOK), TOK),
            pl.ds(pl.multiple_of((j // 2) * GROUP, GROUP), GROUP),
        ] = ref[...]
    for i in range(COLS // 256):
        total[i * 256 : (i + 1) * 256, :] = dot(
            og[:, i * 256 : (i + 1) * 256], att_ref[...], ((0,), (0,))
        ).astype(BF)
    for z in range(NZ):
        for j in range(4):
            base = z * 160 + (j % 2) * SHARD
            lanes = slice((j // 2) * GROUP, (j // 2 + 1) * GROUP)
            first_ref[z, j] = total[base : base + FIRST, lanes]
            rest_ref[j, z] = total[base + FIRST : base + SHARD, lanes]


def attn_grad_body(place, own, other, first, rest, g0, g1, g2, g3, wt_ref, og):
    c, y = place[0], place[1]
    og[pl.ds(pl.multiple_of(c * TOK, TOK), TOK), :] = own[...]
    og[pl.ds(pl.multiple_of((1 - c) * TOK, TOK), TOK), :] = other[...]
    for z in range(NZ):
        for j in range(4):
            base = z * 160 + (j % 2) * SHARD
            lanes = slice((j // 2) * GROUP, (j // 2 + 1) * GROUP)
            wt_ref[base : base + FIRST, lanes] = first[z, j]
            wt_ref[base + FIRST : base + SHARD, lanes] = rest[j, z]
    for k, ref in enumerate((g0, g1, g2, g3)):
        m = (y + k) % 4
        ref[...] = dot(
            og[pl.ds(pl.multiple_of((m % 2) * TOK, TOK), TOK), :],
            wt_ref[:, pl.ds(pl.multiple_of((m // 2) * GROUP, GROUP), GROUP)],
            ((1,), (0,)),
        ).astype(BF)


def layer_out_body(place, att, wt, mine_ref, theirs_ref):
    c = place[0]
    mine_ref[...] = dot(att[pl.ds(pl.multiple_of(c * TOK, TOK), TOK), :], wt[...], ((1,), (1,)))
    theirs_ref[...] = dot(
        att[pl.ds(pl.multiple_of((1 - c) * TOK, TOK), TOK), :], wt[...], ((1,), (1,))
    ).astype(BF)


def sum_x_body(_, blocks, out):
    for z in range(NZ):
        out[z] = (
            (blocks[0, z].astype(F32) + blocks[1, z].astype(F32))
            + (blocks[2, z].astype(F32) + blocks[3, z].astype(F32))
        ).astype(BF)


def sum_z_body(_, first, blocks, out):
    out[:FIRST, :] = first[...]
    total = blocks[0].astype(F32)
    for z in range(1, NZ):
        total = total + blocks[z].astype(F32)
    out[FIRST:, :] = total.astype(BF)


def per_device(query_rows, key_rows, value_matrix, out_weight, out_grad, doc_lengths):
    dp, y = lax.axis_index("dp"), lax.axis_index("mp")
    place = jnp.stack([dp % NC, y]).astype(jnp.int32)
    wt = send(out_weight.T, TO_PLANE)
    rest_w = to_all(to_all(wt[FIRST:], Z_GROUPS), X_GROUPS)
    first_w = gather(to_all(wt[:FIRST], X_GROUPS).reshape(-1, GROUP), Z_GROUPS)
    other_grad = send(out_grad, SWAP)

    attended, prob = call(
        forward_body,
        (shape(TOK, GROUP), shape(HEADS, TOK, TOK, dtype=F32)),
        flops=4 * 4 * TOK * TOK * HEAD,
        moved=2 << 20,
    )(doc_lengths[0], query_rows, key_rows, value_matrix)
    heads = [send(attended, pairs) for pairs in HEADS_OUT]

    big = 2 * 2 * TOK * COLS * 2 * GROUP
    first_part, rest_part, attended_two = call(
        weight_grad_body,
        (shape(NZ, 4, FIRST, GROUP), shape(4, NZ, REST, GROUP), shape(2 * TOK, 2 * GROUP)),
        scratch=(pltpu.VMEM((2 * TOK, COLS), BF), pltpu.VMEM((COLS, 2 * GROUP), BF)),
        flops=big,
        moved=8 << 20,
    )(place, out_grad, other_grad, *heads)

    *partials, wt_two = call(
        attn_grad_body,
        (shape(TOK, GROUP),) * 4 + (shape(COLS, 2 * GROUP),),
        scratch=(pltpu.VMEM((2 * TOK, COLS), BF),),
        flops=big,
        moved=8 << 20,
    )(
        place,
        out_grad,
        other_grad,
        first_w.reshape(NZ, 4, FIRST, GROUP),
        rest_w.reshape(4, NZ, REST, GROUP),
    )
    upstream = [send(partial, pairs) for partial, pairs in zip(partials, HEADS_BACK)]

    mine, theirs = call(
        layer_out_body, (shape(TOK, COLS, dtype=F32), shape(TOK, COLS)), flops=big, moved=6 << 20
    )(place, attended_two, wt_two)
    layer_out = (mine + send(theirs, SWAP).astype(F32)).astype(BF)

    first_sum = scatter(scatter(first_part.reshape(-1, GROUP), Z_GROUPS), X_GROUPS)
    rest_sum = call(sum_x_body, shape(NZ, REST, GROUP), moved=2 << 20)(
        place, exchange(rest_part, X_GROUPS)
    )
    rest_sum = exchange(rest_sum, Z_GROUPS)
    weight_grad = call(sum_z_body, shape(SHARD, GROUP), moved=1 << 20)(place, first_sum, rest_sum)
    weight_grad = send(weight_grad, TO_OWNER).astype(F32)

    query_grad, key_grad, value_grad = call(
        backward_body,
        (shape(TOK, GROUP), shape(TOK, HEAD), shape(TOK, HEAD)),
        flops=5 * 4 * 2 * TOK * TOK * HEAD,
        moved=3 << 20,
    )(place, *upstream, query_rows, key_rows, value_matrix, prob)
    return (layer_out, query_grad, key_grad, value_grad, weight_grad.T)


def solution(mesh):
    placed = (
        P("dp", "mp"),
        P("dp", "mp"),
        P("dp", "mp"),
        P("mp", "dp"),
        P("dp", "mp"),
        P("dp", None),
    )
    return jax.shard_map(
        per_device,
        mesh=mesh,
        in_specs=placed,
        out_specs=(P("dp", "mp"), P("dp", "mp"), P("dp", "mp"), P("dp", "mp"), P("mp", "dp")),
        check_vma=False,
    )
```

```python
import jax
import jax.numpy as jnp
from jax import lax
from jax.experimental import pallas as pl
from jax.experimental.pallas import tpu as pltpu
from jax.sharding import PartitionSpec as P


NX, NZ, NC, NY = 4, 8, 2, 4
HEAD = 128
TOK = 256
HEADS = 4
GROUP = HEADS * HEAD
COLS = 1280
SHARD = 80
AXES = ("dp", "mp")
BF, F32 = jnp.bfloat16, jnp.float32
SCALE = HEAD ** -0.5


def route(target):
    pairs = []
    for x in range(NX):
        for z in range(NZ):
            for c in range(NC):
                for y in range(NY):
                    tx, tz, tc, ty = target(x, z, c, y)
                    src = ((x * NZ + z) * NC + c) * NY + y
                    pairs.append((src, ((tx * NZ + tz) * NC + tc) * NY + ty))
    return pairs


SWAP = route(lambda x, z, c, y: (x, z, 1 - c, y))
TO_PLANE = route(lambda x, z, c, y: (2 * (y % 2) + c, z, y // 2, x))
TO_OWNER = route(lambda x, z, c, y: (y, z, x % 2, 2 * c + x // 2))
HEADS_OUT = [route(lambda x, z, c, y, k=k: (x, z, y // 2, (2 * (y % 2) + c + k) % 4)) for k in range(4)]
HEADS_BACK = [
    route(lambda x, z, c, y, k=k: (x, z, (y + k) % 4 % 2, 2 * c + (y + k) % 4 // 2)) for k in range(4)
]
Z_GROUPS = [[(x * NZ + z) * NC + c for z in range(NZ)] for x in range(NX) for c in range(NC)]
X_GROUPS = [[(x * NZ + z) * NC + c for x in range(NX)] for z in range(NZ) for c in range(NC)]


def send(value, pairs):
    return lax.ppermute(value, AXES, pairs)


def exchange(blocks, groups):
    return lax.all_to_all(blocks, "dp", 0, 0, axis_index_groups=groups, tiled=True)


def scatter(blocks, groups):
    return lax.psum_scatter(blocks, "dp", axis_index_groups=groups, tiled=True)


def to_all(block, groups):
    return exchange(jnp.broadcast_to(block[None], (len(groups[0]), *block.shape)), groups)


def dot(a, b, dims):
    return lax.dot_general(a, b, (dims, ((), ())), preferred_element_type=F32)


def whole(array):
    dims = array.shape
    return pl.BlockSpec(dims, lambda i: (0,) * len(dims), pipeline_mode=pl.Buffered(1))


def call(body, outs, scratch=(), flops=0, moved=0, limit=40):
    def run(scalars, *operands):
        return pl.pallas_call(
            body,
            out_shape=outs,
            grid=(1,),
            in_specs=[pl.BlockSpec(memory_space=pltpu.SMEM)] + [whole(a) for a in operands],
            out_specs=jax.tree.map(whole, outs),
            scratch_shapes=list(scratch),
            compiler_params=pltpu.CompilerParams(vmem_limit_bytes=limit << 20),
            cost_estimate=pl.CostEstimate(flops=flops, bytes_accessed=moved, transcendentals=0),
        )(scalars, *operands)

    return run


def shape(*dims, dtype=BF):
    return jax.ShapeDtypeStruct(dims, dtype)


def forward_body(lengths, q_ref, k_ref, v_ref, att_ref, prob_ref):
    rows = lax.broadcasted_iota(jnp.int32, (TOK, TOK), 0)
    cols = lax.broadcasted_iota(jnp.int32, (TOK, TOK), 1)
    row_at = lax.broadcasted_iota(jnp.int32, (TOK, 1), 0)
    col_at = lax.broadcasted_iota(jnp.int32, (1, TOK), 1)
    row_seg = jnp.zeros((TOK, 1), jnp.int32)
    col_seg = jnp.zeros((1, TOK), jnp.int32)
    end = jnp.int32(0)
    for i in range(8):
        end = end + lengths[i]
        row_seg = row_seg + (row_at >= end).astype(jnp.int32)
        col_seg = col_seg + (col_at >= end).astype(jnp.int32)
    allowed = (row_seg == col_seg) & (rows >= cols)
    for h in range(HEADS):
        at = slice(h * HEAD, (h + 1) * HEAD)
        logits = dot(q_ref[:, at], k_ref[...], ((1,), (1,))) * SCALE
        logits = jnp.where(allowed, logits, -jnp.inf)
        terms = jnp.exp(logits - jnp.max(logits, axis=-1, keepdims=True))
        prob = terms / jnp.sum(terms, axis=-1, keepdims=True)
        prob_ref[h] = prob
        att_ref[:, at] = dot(prob.astype(BF), v_ref[...], ((1,), (0,))).astype(BF)


def backward_body(_, a0, a1, a2, a3, q_ref, k_ref, v_ref, prob_ref, dq_ref, dk_ref, dv_ref):
    key_sum = jnp.zeros((TOK, HEAD), F32)
    value_sum = jnp.zeros((TOK, HEAD), F32)
    for h in range(HEADS):
        at = slice(h * HEAD, (h + 1) * HEAD)
        up = (
            (a0[:, at].astype(F32) + a1[:, at].astype(F32))
            + (a2[:, at].astype(F32) + a3[:, at].astype(F32))
        ).astype(BF)
        prob = prob_ref[h]
        prob_grad = dot(up, v_ref[...], ((1,), (1,)))
        delta = jnp.sum(prob * prob_grad, axis=-1, keepdims=True)
        score = (prob * (prob_grad - delta) * SCALE).astype(BF)
        dq_ref[:, at] = dot(score, k_ref[...], ((1,), (0,))).astype(BF)
        key_sum = key_sum + dot(score, q_ref[:, at], ((0,), (0,)))
        value_sum = value_sum + dot(prob.astype(BF), up, ((0,), (0,)))
    dk_ref[...] = key_sum.astype(BF)
    dv_ref[...] = value_sum.astype(BF)


def weight_grad_body(place, own, other, r0, r1, r2, r3, grad_ref, att_ref, og):
    c, y = place[0], place[1]
    og[pl.ds(pl.multiple_of(c * TOK, TOK), TOK), :] = own[...]
    og[pl.ds(pl.multiple_of((1 - c) * TOK, TOK), TOK), :] = other[...]
    for k, ref in enumerate((r0, r1, r2, r3)):
        j = (y + 4 - k) % 4
        att_ref[
            pl.ds(pl.multiple_of((j % 2) * TOK, TOK), TOK),
            pl.ds(pl.multiple_of((j // 2) * GROUP, GROUP), GROUP),
        ] = ref[...]
    for i in range(COLS // 256):
        grad_ref[i * 256 : (i + 1) * 256, :] = dot(
            og[:, i * 256 : (i + 1) * 256], att_ref[...], ((0,), (0,))
        ).astype(BF)


def attn_grad_body(place, own, other, blocks, g0, g1, g2, g3, wt_ref, og):
    c, y = place[0], place[1]
    og[pl.ds(pl.multiple_of(c * TOK, TOK), TOK), :] = own[...]
    og[pl.ds(pl.multiple_of((1 - c) * TOK, TOK), TOK), :] = other[...]
    for z in range(NZ):
        for j in range(4):
            base = z * 160 + (j % 2) * SHARD
            wt_ref[base : base + SHARD, (j // 2) * GROUP : (j // 2 + 1) * GROUP] = blocks[j, z]
    for k, ref in enumerate((g0, g1, g2, g3)):
        m = (y + k) % 4
        ref[...] = dot(
            og[pl.ds(pl.multiple_of((m % 2) * TOK, TOK), TOK), :],
            wt_ref[:, pl.ds(pl.multiple_of((m // 2) * GROUP, GROUP), GROUP)],
            ((1,), (0,)),
        ).astype(BF)


def layer_out_body(place, att, wt, mine_ref, theirs_ref):
    c = place[0]
    mine_ref[...] = dot(att[pl.ds(pl.multiple_of(c * TOK, TOK), TOK), :], wt[...], ((1,), (1,)))
    theirs_ref[...] = dot(
        att[pl.ds(pl.multiple_of((1 - c) * TOK, TOK), TOK), :], wt[...], ((1,), (1,))
    ).astype(BF)


def sum_x_body(_, blocks, out):
    out[...] = (
        (blocks[0].astype(F32) + blocks[1].astype(F32))
        + (blocks[2].astype(F32) + blocks[3].astype(F32))
    ).astype(BF)


def split_body(_, rows, out):
    for j in range(4):
        out[j] = rows[(j % 2) * SHARD : (j % 2 + 1) * SHARD, (j // 2) * GROUP : (j // 2 + 1) * GROUP]


def per_device(query_rows, key_rows, value_matrix, out_weight, out_grad, doc_lengths):
    dp, y = lax.axis_index("dp"), lax.axis_index("mp")
    place = jnp.stack([dp % NC, y]).astype(jnp.int32)
    wt = send(out_weight.T, TO_PLANE)
    blocks = to_all(to_all(wt, Z_GROUPS), X_GROUPS)
    other_grad = send(out_grad, SWAP)

    attended, prob = call(
        forward_body,
        (shape(TOK, GROUP), shape(HEADS, TOK, TOK, dtype=F32)),
        flops=4 * 4 * TOK * TOK * HEAD,
        moved=2 << 20,
        limit=63,
    )(doc_lengths[0], query_rows, key_rows, value_matrix)
    heads = [send(attended, pairs) for pairs in HEADS_OUT]

    big = 2 * 2 * TOK * COLS * 2 * GROUP
    grad_part, attended_two = call(
        weight_grad_body,
        (shape(COLS, 2 * GROUP), shape(2 * TOK, 2 * GROUP)),
        scratch=(pltpu.VMEM((2 * TOK, COLS), BF),),
        flops=big,
        moved=8 << 20,
    )(place, out_grad, other_grad, *heads)
    grad_rows = scatter(grad_part, Z_GROUPS)

    *partials, wt_two = call(
        attn_grad_body,
        (shape(TOK, GROUP),) * 4 + (shape(COLS, 2 * GROUP),),
        scratch=(pltpu.VMEM((2 * TOK, COLS), BF),),
        flops=big,
        moved=8 << 20,
    )(place, out_grad, other_grad, blocks)
    upstream = [send(partial, pairs) for partial, pairs in zip(partials, HEADS_BACK)]

    mine, theirs = call(
        layer_out_body, (shape(TOK, COLS, dtype=F32), shape(TOK, COLS)), flops=big, moved=6 << 20
    )(place, attended_two, wt_two)
    theirs = send(theirs, SWAP)
    layer_out = (mine + theirs.astype(F32)).astype(BF)

    pieces = call(split_body, shape(4, SHARD, GROUP), moved=1 << 20)(place, grad_rows)
    weight_grad = call(sum_x_body, shape(SHARD, GROUP), moved=1 << 20)(
        place, exchange(pieces, X_GROUPS)
    )
    weight_grad = send(weight_grad, TO_OWNER).astype(F32)

    query_grad, key_grad, value_grad = call(
        backward_body,
        (shape(TOK, GROUP), shape(TOK, HEAD), shape(TOK, HEAD)),
        flops=5 * 4 * 2 * TOK * TOK * HEAD,
        moved=3 << 20,
        limit=63,
    )(place, *upstream, query_rows, key_rows, value_matrix, prob)
    return (layer_out, query_grad, key_grad, value_grad, weight_grad.T)


def solution(mesh):
    placed = (
        P("dp", "mp"),
        P("dp", "mp"),
        P("dp", "mp"),
        P("mp", "dp"),
        P("dp", "mp"),
        P("dp", None),
    )
    return jax.shard_map(
        per_device,
        mesh=mesh,
        in_specs=placed,
        out_specs=(P("dp", "mp"), P("dp", "mp"), P("dp", "mp"), P("dp", "mp"), P("mp", "dp")),
        check_vma=False,
    )
```

```python
import jax
import jax.numpy as jnp
from jax import lax
from jax.experimental import pallas as pl
from jax.experimental.pallas import tpu as pltpu
from jax.sharding import PartitionSpec as P


NX, NZ, NC, NY = 4, 8, 2, 4
HEAD = 128
TOK = 256
HEADS = 4
GROUP = HEADS * HEAD
COLS = 1280
SHARD = 80
AXES = ("dp", "mp")
BF, F32 = jnp.bfloat16, jnp.float32
SCALE = HEAD ** -0.5


def route(target):
    pairs = []
    for x in range(NX):
        for z in range(NZ):
            for c in range(NC):
                for y in range(NY):
                    tx, tz, tc, ty = target(x, z, c, y)
                    src = ((x * NZ + z) * NC + c) * NY + y
                    pairs.append((src, ((tx * NZ + tz) * NC + tc) * NY + ty))
    return pairs


SWAP = route(lambda x, z, c, y: (x, z, 1 - c, y))
ACROSS = route(lambda x, z, c, y: (x ^ 1, z, c, y))
TO_PLANE = [
    route(lambda x, z, c, y, k=k: (2 * ((c + k) % 2) + y // 2, z, y % 2, x)) for k in range(2)
]
TO_OWNER = [
    route(lambda x, z, c, y, k=k: (y, z, (x // 2 + k) % 2, 2 * (x % 2) + c)) for k in range(2)
]
HEADS_OUT = [
    route(lambda x, z, c, y, k=k: (x // 2 * 2 + y // 2, z, y % 2, (2 * (x % 2) + c + k) % 4))
    for k in range(4)
]
HEADS_BACK = [
    route(lambda x, z, c, y, k=k: (x // 2 * 2 + (y + k) % 4 // 2, z, (y + k) % 2, 2 * (x % 2) + c))
    for k in range(4)
]
Z_GROUPS = [[(x * NZ + z) * NC + c for z in range(NZ)] for x in range(NX) for c in range(NC)]


def send(value, pairs):
    return lax.ppermute(value, AXES, pairs)


def exchange(blocks, groups):
    return lax.all_to_all(blocks, "dp", 0, 0, axis_index_groups=groups, tiled=True)


def dot(a, b, dims):
    return lax.dot_general(a, b, (dims, ((), ())), preferred_element_type=F32)


def whole(array):
    dims = array.shape
    return pl.BlockSpec(dims, lambda i: (0,) * len(dims), pipeline_mode=pl.Buffered(1))


def call(body, outs, scratch=(), flops=0, moved=0, limit=63):
    def run(scalars, *operands):
        return pl.pallas_call(
            body,
            out_shape=outs,
            grid=(1,),
            in_specs=[pl.BlockSpec(memory_space=pltpu.SMEM)] + [whole(a) for a in operands],
            out_specs=jax.tree.map(whole, outs),
            scratch_shapes=list(scratch),
            compiler_params=pltpu.CompilerParams(vmem_limit_bytes=limit << 20),
            cost_estimate=pl.CostEstimate(flops=flops, bytes_accessed=moved, transcendentals=0),
        )(scalars, *operands)

    return run


def shape(*dims, dtype=BF):
    return jax.ShapeDtypeStruct(dims, dtype)


def forward_body(lengths, q_ref, k_ref, v_ref, att_ref, prob_ref):
    rows = lax.broadcasted_iota(jnp.int32, (TOK, TOK), 0)
    cols = lax.broadcasted_iota(jnp.int32, (TOK, TOK), 1)
    row_at = lax.broadcasted_iota(jnp.int32, (TOK, 1), 0)
    col_at = lax.broadcasted_iota(jnp.int32, (1, TOK), 1)
    row_seg = jnp.zeros((TOK, 1), jnp.int32)
    col_seg = jnp.zeros((1, TOK), jnp.int32)
    end = jnp.int32(0)
    for i in range(8):
        end = end + lengths[i]
        row_seg = row_seg + (row_at >= end).astype(jnp.int32)
        col_seg = col_seg + (col_at >= end).astype(jnp.int32)
    allowed = (row_seg == col_seg) & (rows >= cols)
    for h in range(HEADS):
        at = slice(h * HEAD, (h + 1) * HEAD)
        logits = dot(q_ref[:, at], k_ref[...], ((1,), (1,))) * SCALE
        logits = jnp.where(allowed, logits, -jnp.inf)
        terms = jnp.exp(logits - jnp.max(logits, axis=-1, keepdims=True))
        prob = terms / jnp.sum(terms, axis=-1, keepdims=True)
        prob_ref[h] = prob
        att_ref[:, at] = dot(prob.astype(BF), v_ref[...], ((1,), (0,))).astype(BF)


def backward_body(_, a0, a1, a2, a3, q_ref, k_ref, v_ref, prob_ref, dq_ref, dk_ref, dv_ref):
    key_sum = jnp.zeros((TOK, HEAD), F32)
    value_sum = jnp.zeros((TOK, HEAD), F32)
    for h in range(HEADS):
        at = slice(h * HEAD, (h + 1) * HEAD)
        up = (
            (a0[:, at].astype(F32) + a1[:, at].astype(F32))
            + (a2[:, at].astype(F32) + a3[:, at].astype(F32))
        ).astype(BF)
        prob = prob_ref[h]
        prob_grad = dot(up, v_ref[...], ((1,), (1,)))
        delta = jnp.sum(prob * prob_grad, axis=-1, keepdims=True)
        score = (prob * (prob_grad - delta) * SCALE).astype(BF)
        dq_ref[:, at] = dot(score, k_ref[...], ((1,), (0,))).astype(BF)
        key_sum = key_sum + dot(score, q_ref[:, at], ((0,), (0,)))
        value_sum = value_sum + dot(prob.astype(BF), up, ((0,), (0,)))
    dk_ref[...] = key_sum.astype(BF)
    dv_ref[...] = value_sum.astype(BF)


def weight_grad_body(place, o0, o1, o2, o3, r0, r1, r2, r3, grad_ref, att_ref):
    g, y = place[0], place[1]
    for k, ref in enumerate((r0, r1, r2, r3)):
        att_ref[jnp.bitwise_xor((y + 4 - k) % 4, g)] = ref[...]
    for i in range(COLS // 256):
        at = slice(i * 256, (i + 1) * 256)
        total = dot(o0[:, at], att_ref[0], ((0,), (0,)))
        for r, ref in ((1, o1), (2, o2), (3, o3)):
            total = total + dot(ref[:, at], att_ref[r], ((0,), (0,)))
        grad_ref[at, :] = total.astype(BF)


def layer_out_body(place, att, w0, w1, mine_ref, across_ref, pair_ref, wt_ref):
    high = place[2]
    for k, ref in enumerate((w0, w1)):
        c = (high + k) % 2
        for z in range(NZ):
            wt_ref[pl.ds(pl.multiple_of(z * 160 + c * SHARD, 16), SHARD), :] = ref[z]
    pair_ref[0] = dot(att[1], wt_ref[...], ((1,), (1,))).astype(BF)
    pair_ref[1] = dot(att[3], wt_ref[...], ((1,), (1,))).astype(BF)
    across_ref[...] = dot(att[2], wt_ref[...], ((1,), (1,)))
    mine_ref[...] = dot(att[0], wt_ref[...], ((1,), (1,)))


def attn_grad_body(place, o0, o1, o2, o3, wt, g0, g1, g2, g3, og):
    g, y = place[0], place[1]
    for r, ref in enumerate((o0, o1, o2, o3)):
        og[r] = ref[...]
    for k, ref in enumerate((g0, g1, g2, g3)):
        at = jnp.bitwise_xor((y + k) % 4, g)
        ref[...] = dot(og[at], wt[...], ((1,), (0,))).astype(BF)


def sum_z_body(place, blocks, o0, o1):
    high = place[2]
    for k, ref in enumerate((o0, o1)):
        at = pl.ds(pl.multiple_of((high + k) % 2 * SHARD, 16), SHARD)
        total = blocks[0, at, :].astype(F32)
        for z in range(1, NZ):
            total = total + blocks[z, at, :].astype(F32)
        ref[...] = total.astype(BF)


def per_device(query_rows, key_rows, value_matrix, out_weight, out_grad, doc_lengths):
    dp, y = lax.axis_index("dp"), lax.axis_index("mp")
    x = dp // (NZ * NC)
    place = jnp.stack([2 * (x % 2) + dp % NC, y, x // 2]).astype(jnp.int32)
    across_grad = send(out_grad, ACROSS)
    cols = [out_grad, send(out_grad, SWAP), across_grad, send(across_grad, SWAP)]

    wt = jnp.broadcast_to(out_weight.T[None], (NZ, SHARD, GROUP))
    wt = exchange(wt, Z_GROUPS)
    blocks = [send(wt, pairs) for pairs in TO_PLANE]

    attended, prob = call(
        forward_body,
        (shape(TOK, GROUP), shape(HEADS, TOK, TOK, dtype=F32)),
        flops=4 * 4 * TOK * TOK * HEAD,
        moved=2 << 20,
    )(doc_lengths[0], query_rows, key_rows, value_matrix)
    heads = [send(attended, pairs) for pairs in HEADS_OUT]

    big = 2 * 4 * TOK * COLS * GROUP
    grad_part, attended_all = call(
        weight_grad_body, (shape(COLS, GROUP), shape(4, TOK, GROUP)), flops=big, moved=6 << 20
    )(place, *cols, *heads)
    grad_rows = exchange(grad_part.reshape(NZ, 2 * SHARD, GROUP), Z_GROUPS)

    mine, across, pair, wt_all = call(
        layer_out_body,
        (shape(TOK, COLS, dtype=F32), shape(TOK, COLS, dtype=F32), shape(2, TOK, COLS), shape(COLS, GROUP)),
        flops=big,
        moved=8 << 20,
    )(place, attended_all, *blocks)
    pair = send(pair, SWAP)
    across = (across + pair[1].astype(F32)).astype(BF)
    across = send(across, ACROSS)
    layer_out = (mine + pair[0].astype(F32) + across.astype(F32)).astype(BF)

    partials = call(
        attn_grad_body,
        (shape(TOK, GROUP),) * 4,
        scratch=(pltpu.VMEM((4, TOK, COLS), BF),),
        flops=big,
        moved=6 << 20,
    )(place, *cols, wt_all)
    upstream = [send(partial, pairs) for partial, pairs in zip(partials, HEADS_BACK)]

    query_grad, key_grad, value_grad = call(
        backward_body,
        (shape(TOK, GROUP), shape(TOK, HEAD), shape(TOK, HEAD)),
        flops=5 * 4 * 2 * TOK * TOK * HEAD,
        moved=3 << 20,
    )(place, *upstream, query_rows, key_rows, value_matrix, prob)

    pieces = call(sum_z_body, (shape(SHARD, GROUP),) * 2, moved=2 << 20)(place, grad_rows)
    pieces = [send(piece, pairs).astype(F32) for piece, pairs in zip(pieces, TO_OWNER)]
    weight_grad = pieces[0] + pieces[1]
    return (layer_out, query_grad, key_grad, value_grad, weight_grad.T)


def solution(mesh):
    placed = (
        P("dp", "mp"),
        P("dp", "mp"),
        P("dp", "mp"),
        P("mp", "dp"),
        P("dp", "mp"),
        P("dp", None),
    )
    return jax.shard_map(
        per_device,
        mesh=mesh,
        in_specs=placed,
        out_specs=(P("dp", "mp"), P("dp", "mp"), P("dp", "mp"), P("dp", "mp"), P("mp", "dp")),
        check_vma=False,
    )
```

```python
import jax
import jax.numpy as jnp
from jax import lax
from jax.experimental import pallas as pl
from jax.experimental.pallas import tpu as pltpu
from jax.sharding import PartitionSpec as P


NX, NZ, NC, NY = 4, 8, 2, 4
HEAD = 128
TOK = 256
HEADS = 4
GROUP = HEADS * HEAD
COLS = 1280
SHARD = 80
AXES = ("dp", "mp")
BF, F32 = jnp.bfloat16, jnp.float32
SCALE = HEAD ** -0.5


def route(target):
    pairs = []
    for x in range(NX):
        for z in range(NZ):
            for c in range(NC):
                for y in range(NY):
                    tx, tz, tc, ty = target(x, z, c, y)
                    src = ((x * NZ + z) * NC + c) * NY + y
                    pairs.append((src, ((tx * NZ + tz) * NC + tc) * NY + ty))
    return pairs


def low_of(x):
    return (x + x // 2) % 2


def chip(high, low):
    return 3 - low if high else low


SWAP = route(lambda x, z, c, y: (x, z, 1 - c, y))
ACROSS = route(lambda x, z, c, y: (x ^ 1, z, c, y))
OTHER = route(lambda x, z, c, y: (3 - x, z, c, y))
TO_PLANE = route(lambda x, z, c, y: (chip(c, y // 2), z, y % 2, x))
TO_OWNER = [
    route(lambda x, z, c, y, k=k: (y, z, (x // 2 + k) % 2, 2 * low_of(x) + c)) for k in range(2)
]
HEADS_OUT = [
    route(lambda x, z, c, y, k=k: (chip(x // 2, y // 2), z, y % 2, (2 * low_of(x) + c + k) % 4))
    for k in range(4)
]
HEADS_BACK = [
    route(lambda x, z, c, y, k=k: (chip(x // 2, (y + k) % 4 // 2), z, (y + k) % 2, 2 * low_of(x) + c))
    for k in range(4)
]
Z_GROUPS = [[(x * NZ + z) * NC + c for z in range(NZ)] for x in range(NX) for c in range(NC)]


def send(value, pairs):
    return lax.ppermute(value, AXES, pairs)


def exchange(blocks, groups):
    return lax.all_to_all(blocks, "dp", 0, 0, axis_index_groups=groups, tiled=True)


def dot(a, b, dims):
    return lax.dot_general(a, b, (dims, ((), ())), preferred_element_type=F32)


def whole(array):
    dims = array.shape
    return pl.BlockSpec(dims, lambda i: (0,) * len(dims), pipeline_mode=pl.Buffered(1))


def call(body, outs, scratch=(), flops=0, moved=0, limit=12):
    def run(scalars, *operands):
        return pl.pallas_call(
            body,
            out_shape=outs,
            grid=(1,),
            in_specs=[pl.BlockSpec(memory_space=pltpu.SMEM)] + [whole(a) for a in operands],
            out_specs=jax.tree.map(whole, outs),
            scratch_shapes=list(scratch),
            compiler_params=pltpu.CompilerParams(vmem_limit_bytes=limit << 20),
            cost_estimate=pl.CostEstimate(flops=flops, bytes_accessed=moved, transcendentals=0),
        )(scalars, *operands)

    return run


def shape(*dims, dtype=BF):
    return jax.ShapeDtypeStruct(dims, dtype)


def forward_body(lengths, q_ref, k_ref, v_ref, att_ref, prob_ref):
    rows = lax.broadcasted_iota(jnp.int32, (TOK, TOK), 0)
    cols = lax.broadcasted_iota(jnp.int32, (TOK, TOK), 1)
    row_at = lax.broadcasted_iota(jnp.int32, (TOK, 1), 0)
    col_at = lax.broadcasted_iota(jnp.int32, (1, TOK), 1)
    row_seg = jnp.zeros((TOK, 1), jnp.int32)
    col_seg = jnp.zeros((1, TOK), jnp.int32)
    end = jnp.int32(0)
    for i in range(8):
        end = end + lengths[i]
        row_seg = row_seg + (row_at >= end).astype(jnp.int32)
        col_seg = col_seg + (col_at >= end).astype(jnp.int32)
    allowed = (row_seg == col_seg) & (rows >= cols)
    for h in range(HEADS):
        at = slice(h * HEAD, (h + 1) * HEAD)
        logits = dot(q_ref[:, at], k_ref[...], ((1,), (1,))) * SCALE
        logits = jnp.where(allowed, logits, -jnp.inf)
        terms = jnp.exp(logits - jnp.max(logits, axis=-1, keepdims=True))
        prob = terms / jnp.sum(terms, axis=-1, keepdims=True)
        prob_ref[h] = prob
        att_ref[:, at] = dot(prob.astype(BF), v_ref[...], ((1,), (0,))).astype(BF)


def backward_body(_, a0, a1, a2, a3, q_ref, k_ref, v_ref, prob_ref, dq_ref, dk_ref, dv_ref):
    key_sum = jnp.zeros((TOK, HEAD), F32)
    value_sum = jnp.zeros((TOK, HEAD), F32)
    for h in range(HEADS):
        at = slice(h * HEAD, (h + 1) * HEAD)
        up = (
            (a0[:, at].astype(F32) + a1[:, at].astype(F32))
            + (a2[:, at].astype(F32) + a3[:, at].astype(F32))
        ).astype(BF)
        prob = prob_ref[h]
        prob_grad = dot(up, v_ref[...], ((1,), (1,)))
        delta = jnp.sum(prob * prob_grad, axis=-1, keepdims=True)
        score = (prob * (prob_grad - delta) * SCALE).astype(BF)
        dq_ref[:, at] = dot(score, k_ref[...], ((1,), (0,))).astype(BF)
        key_sum = key_sum + dot(score, q_ref[:, at], ((0,), (0,)))
        value_sum = value_sum + dot(prob.astype(BF), up, ((0,), (0,)))
    dk_ref[...] = key_sum.astype(BF)
    dv_ref[...] = value_sum.astype(BF)


def weight_grad_body(place, o0, o1, o2, o3, r0, r1, r2, r3, grad_ref, att):
    g, y = place[0], place[1]
    for k, ref in enumerate((r0, r1, r2, r3)):
        att[jnp.bitwise_xor((y + 4 - k) % 4, g)] = ref[...]
    for i in range(COLS // 256):
        at = slice(i * 256, (i + 1) * 256)
        total = dot(o0[:, at], att[0], ((0,), (0,)))
        for r, ref in ((1, o1), (2, o2), (3, o3)):
            total = total + dot(ref[:, at], att[r], ((0,), (0,)))
        grad_ref[at, :] = total.astype(BF)


def layer_pair_body(place, r0, r1, r2, r3, w0, w1, pair_ref, att_ref, wt_ref, att):
    g, y, high = place[0], place[1], place[2]
    for k, ref in enumerate((r0, r1, r2, r3)):
        att[jnp.bitwise_xor((y + 4 - k) % 4, g)] = ref[...]
    for k, ref in enumerate((w0, w1)):
        c = (high + k) % 2
        for z in range(NZ):
            wt_ref[pl.ds(pl.multiple_of(z * 160 + c * SHARD, 16), SHARD), :] = ref[z]
    for i in range(2):
        pair_ref[i] = dot(att[2 * i + 1], wt_ref[...], ((1,), (1,))).astype(BF)
        att_ref[i] = att[2 * i]


def layer_across_body(_, att, wt, pair, out):
    out[...] = (dot(att[1], wt[...], ((1,), (1,))) + pair[1].astype(F32)).astype(BF)


def layer_sum_body(_, att, wt, pair, across, out):
    out[...] = (
        dot(att[0], wt[...], ((1,), (1,))) + pair[0].astype(F32) + across[...].astype(F32)
    ).astype(BF)


def attn_grad_body(place, o0, o1, o2, o3, wt, g0, g1, g2, g3, og):
    g, y = place[0], place[1]
    for r, ref in enumerate((o0, o1, o2, o3)):
        og[r] = ref[...]
    for k, ref in enumerate((g0, g1, g2, g3)):
        at = jnp.bitwise_xor((y + k) % 4, g)
        ref[...] = dot(og[at], wt[...], ((1,), (0,))).astype(BF)


def sum_z_body(place, blocks, o0, o1):
    high = place[2]
    for k, ref in enumerate((o0, o1)):
        at = pl.ds(pl.multiple_of((high + k) % 2 * SHARD, 16), SHARD)
        total = blocks[0, at, :].astype(F32)
        for z in range(1, NZ):
            total = total + blocks[z, at, :].astype(F32)
        ref[...] = total.astype(BF)


def per_device(query_rows, key_rows, value_matrix, out_weight, out_grad, doc_lengths):
    dp, y = lax.axis_index("dp"), lax.axis_index("mp")
    x = dp // (NZ * NC)
    place = jnp.stack([2 * low_of(x) + dp % NC, y, x // 2]).astype(jnp.int32)
    across_grad = send(out_grad, ACROSS)
    cols = [out_grad, send(out_grad, SWAP), across_grad, send(across_grad, SWAP)]

    wt = send(out_weight.T, TO_PLANE)
    wt = exchange(jnp.broadcast_to(wt[None], (NZ, SHARD, GROUP)), Z_GROUPS)
    blocks = [wt, send(wt, OTHER)]

    attended, prob = call(
        forward_body,
        (shape(TOK, GROUP), shape(HEADS, TOK, TOK, dtype=F32)),
        flops=4 * 4 * TOK * TOK * HEAD,
        moved=2 << 20,
    )(doc_lengths[0], query_rows, key_rows, value_matrix)
    heads = [send(attended, pairs) for pairs in HEADS_OUT]

    big = 2 * 4 * TOK * COLS * GROUP
    grad_part = call(
        weight_grad_body,
        shape(COLS, GROUP),
        scratch=(pltpu.VMEM((4, TOK, GROUP), BF),),
        flops=big,
        moved=6 << 20,
    )(place, *cols, *heads)
    grad_rows = exchange(grad_part.reshape(NZ, 2 * SHARD, GROUP), Z_GROUPS)

    pair, attended_two, wt_all = call(
        layer_pair_body,
        (shape(2, TOK, COLS), shape(2, TOK, GROUP), shape(COLS, GROUP)),
        scratch=(pltpu.VMEM((4, TOK, GROUP), BF),),
        flops=big // 2,
        moved=6 << 20,
    )(place, *heads, *blocks)
    pair = send(pair, SWAP)
    across = call(
        layer_across_body, shape(TOK, COLS), flops=big // 4, moved=3 << 20
    )(place, attended_two, wt_all, pair)
    across = send(across, ACROSS)
    layer_out = call(
        layer_sum_body, shape(TOK, COLS), flops=big // 4, moved=4 << 20
    )(place, attended_two, wt_all, pair, across)

    partials = call(
        attn_grad_body,
        (shape(TOK, GROUP),) * 4,
        scratch=(pltpu.VMEM((4, TOK, COLS), BF),),
        flops=big,
        moved=6 << 20,
    )(place, *cols, wt_all)
    upstream = [send(partial, pairs) for partial, pairs in zip(partials, HEADS_BACK)]

    query_grad, key_grad, value_grad = call(
        backward_body,
        (shape(TOK, GROUP), shape(TOK, HEAD), shape(TOK, HEAD)),
        flops=5 * 4 * 2 * TOK * TOK * HEAD,
        moved=3 << 20,
    )(place, *upstream, query_rows, key_rows, value_matrix, prob)

    pieces = call(sum_z_body, (shape(SHARD, GROUP),) * 2, moved=2 << 20)(place, grad_rows)
    pieces = [send(piece, pairs).astype(F32) for piece, pairs in zip(pieces, TO_OWNER)]
    weight_grad = pieces[0] + pieces[1]
    return (layer_out, query_grad, key_grad, value_grad, weight_grad.T)


def solution(mesh):
    placed = (
        P("dp", "mp"),
        P("dp", "mp"),
        P("dp", "mp"),
        P("mp", "dp"),
        P("dp", "mp"),
        P("dp", None),
    )
    return jax.shard_map(
        per_device,
        mesh=mesh,
        in_specs=placed,
        out_specs=(P("dp", "mp"), P("dp", "mp"), P("dp", "mp"), P("dp", "mp"), P("mp", "dp")),
        check_vma=False,
    )
```

```python
import jax
import jax.numpy as jnp
from jax import lax
from jax.experimental import pallas as pl
from jax.experimental.pallas import tpu as pltpu
from jax.sharding import PartitionSpec as P


NX, NZ, NC, NY = 4, 8, 2, 4
HEAD = 128
TOK = 256
HEADS = 4
GROUP = HEADS * HEAD
COLS = 1280
SHARD = 80
AXES = ("dp", "mp")
BF, F32 = jnp.bfloat16, jnp.float32
SCALE = HEAD ** -0.5


def route(target):
    pairs = []
    for x in range(NX):
        for z in range(NZ):
            for c in range(NC):
                for y in range(NY):
                    tx, tz, tc, ty = target(x, z, c, y)
                    src = ((x * NZ + z) * NC + c) * NY + y
                    pairs.append((src, ((tx * NZ + tz) * NC + tc) * NY + ty))
    return pairs


def low_of(x):
    return (x + x // 2) % 2


def chip(high, low):
    return 3 - low if high else low


SWAP = route(lambda x, z, c, y: (x, z, 1 - c, y))
ACROSS = route(lambda x, z, c, y: (x ^ 1, z, c, y))
OTHER = route(lambda x, z, c, y: (3 - x, z, c, y))
TO_PLANE = route(lambda x, z, c, y: (chip(c, y // 2), z, y % 2, x))
TO_OWNER = [
    route(lambda x, z, c, y, k=k: (y, z, (x // 2 + k) % 2, 2 * low_of(x) + c)) for k in range(2)
]
TURN = route(lambda x, z, c, y: (chip(x // 2, y // 2), z, y % 2, 2 * low_of(x) + c))
ALONG_Y = [route(lambda x, z, c, y, k=k: (x, z, c, (y + k) % 4)) for k in range(1, 4)]
Z_GROUPS = [[(x * NZ + z) * NC + c for z in range(NZ)] for x in range(NX) for c in range(NC)]


def send(value, pairs):
    return lax.ppermute(value, AXES, pairs)


def exchange(blocks, groups):
    return lax.all_to_all(blocks, "dp", 0, 0, axis_index_groups=groups, tiled=True)


def dot(a, b, dims):
    return lax.dot_general(a, b, (dims, ((), ())), preferred_element_type=F32)


def whole(array):
    dims = array.shape
    return pl.BlockSpec(dims, lambda i: (0,) * len(dims), pipeline_mode=pl.Buffered(1))


def call(body, outs, scratch=(), flops=0, moved=0, limit=12):
    def run(scalars, *operands):
        return pl.pallas_call(
            body,
            out_shape=outs,
            grid=(1,),
            in_specs=[pl.BlockSpec(memory_space=pltpu.SMEM)] + [whole(a) for a in operands],
            out_specs=jax.tree.map(whole, outs),
            scratch_shapes=list(scratch),
            compiler_params=pltpu.CompilerParams(vmem_limit_bytes=limit << 20),
            cost_estimate=pl.CostEstimate(flops=flops, bytes_accessed=moved, transcendentals=0),
        )(scalars, *operands)

    return run


def shape(*dims, dtype=BF):
    return jax.ShapeDtypeStruct(dims, dtype)


def forward_body(lengths, q_ref, k_ref, v_ref, att_ref, prob_ref):
    rows = lax.broadcasted_iota(jnp.int32, (TOK, TOK), 0)
    cols = lax.broadcasted_iota(jnp.int32, (TOK, TOK), 1)
    row_at = lax.broadcasted_iota(jnp.int32, (TOK, 1), 0)
    col_at = lax.broadcasted_iota(jnp.int32, (1, TOK), 1)
    row_seg = jnp.zeros((TOK, 1), jnp.int32)
    col_seg = jnp.zeros((1, TOK), jnp.int32)
    end = jnp.int32(0)
    for i in range(8):
        end = end + lengths[i]
        row_seg = row_seg + (row_at >= end).astype(jnp.int32)
        col_seg = col_seg + (col_at >= end).astype(jnp.int32)
    allowed = (row_seg == col_seg) & (rows >= cols)
    for h in range(HEADS):
        at = slice(h * HEAD, (h + 1) * HEAD)
        logits = dot(q_ref[:, at], k_ref[...], ((1,), (1,))) * SCALE
        logits = jnp.where(allowed, logits, -jnp.inf)
        terms = jnp.exp(logits - jnp.max(logits, axis=-1, keepdims=True))
        prob = terms / jnp.sum(terms, axis=-1, keepdims=True)
        prob_ref[h] = prob
        att_ref[:, at] = dot(prob.astype(BF), v_ref[...], ((1,), (0,))).astype(BF)


def sum_four_body(_, a0, a1, a2, a3, out):
    out[...] = (
        (a0[...].astype(F32) + a1[...].astype(F32)) + (a2[...].astype(F32) + a3[...].astype(F32))
    ).astype(BF)


def backward_body(_, up_ref, q_ref, k_ref, v_ref, prob_ref, dq_ref, dk_ref, dv_ref):
    key_sum = jnp.zeros((TOK, HEAD), F32)
    value_sum = jnp.zeros((TOK, HEAD), F32)
    for h in range(HEADS):
        at = slice(h * HEAD, (h + 1) * HEAD)
        up = up_ref[:, at]
        prob = prob_ref[h]
        prob_grad = dot(up, v_ref[...], ((1,), (1,)))
        delta = jnp.sum(prob * prob_grad, axis=-1, keepdims=True)
        score = (prob * (prob_grad - delta) * SCALE).astype(BF)
        dq_ref[:, at] = dot(score, k_ref[...], ((1,), (0,))).astype(BF)
        key_sum = key_sum + dot(score, q_ref[:, at], ((0,), (0,)))
        value_sum = value_sum + dot(prob.astype(BF), up, ((0,), (0,)))
    dk_ref[...] = key_sum.astype(BF)
    dv_ref[...] = value_sum.astype(BF)


def weight_grad_body(place, o0, o1, o2, o3, r0, r1, r2, r3, grad_ref, att):
    g, y = place[0], place[1]
    for k, ref in enumerate((r0, r1, r2, r3)):
        att[jnp.bitwise_xor((y + 4 - k) % 4, g)] = ref[...]
    for i in range(COLS // 256):
        at = slice(i * 256, (i + 1) * 256)
        total = dot(o0[:, at], att[0], ((0,), (0,)))
        for r, ref in ((1, o1), (2, o2), (3, o3)):
            total = total + dot(ref[:, at], att[r], ((0,), (0,)))
        grad_ref[at, :] = total.astype(BF)


def layer_pair_body(place, r0, r1, r2, r3, w0, w1, pair_ref, att_ref, wt_ref, att):
    g, y, high = place[0], place[1], place[2]
    for k, ref in enumerate((r0, r1, r2, r3)):
        att[jnp.bitwise_xor((y + 4 - k) % 4, g)] = ref[...]
    for k, ref in enumerate((w0, w1)):
        c = (high + k) % 2
        for z in range(NZ):
            wt_ref[pl.ds(pl.multiple_of(z * 160 + c * SHARD, 16), SHARD), :] = ref[z]
    for i in range(2):
        pair_ref[i] = dot(att[2 * i + 1], wt_ref[...], ((1,), (1,))).astype(BF)
        att_ref[i] = att[2 * i]


def layer_across_body(_, att, wt, pair, out):
    out[...] = (dot(att[1], wt[...], ((1,), (1,))) + pair[1].astype(F32)).astype(BF)


def layer_sum_body(_, att, wt, pair, across, out):
    out[...] = (
        dot(att[0], wt[...], ((1,), (1,))) + pair[0].astype(F32) + across[...].astype(F32)
    ).astype(BF)


def attn_grad_body(place, o0, o1, o2, o3, wt, g0, g1, g2, g3, og):
    g, y = place[0], place[1]
    for r, ref in enumerate((o0, o1, o2, o3)):
        og[r] = ref[...]
    for k, ref in enumerate((g0, g1, g2, g3)):
        at = jnp.bitwise_xor((y + k) % 4, g)
        ref[...] = dot(og[at], wt[...], ((1,), (0,))).astype(BF)


def sum_z_body(place, blocks, o0, o1):
    high = place[2]
    for k, ref in enumerate((o0, o1)):
        at = pl.ds(pl.multiple_of((high + k) % 2 * SHARD, 16), SHARD)
        total = blocks[0, at, :].astype(F32)
        for z in range(1, NZ):
            total = total + blocks[z, at, :].astype(F32)
        ref[...] = total.astype(BF)


def per_device(query_rows, key_rows, value_matrix, out_weight, out_grad, doc_lengths):
    dp, y = lax.axis_index("dp"), lax.axis_index("mp")
    x = dp // (NZ * NC)
    place = jnp.stack([2 * low_of(x) + dp % NC, y, x // 2]).astype(jnp.int32)
    across_grad = send(out_grad, ACROSS)
    cols = [out_grad, send(out_grad, SWAP), across_grad, send(across_grad, SWAP)]

    wt = send(out_weight.T, TO_PLANE)
    wt = exchange(jnp.broadcast_to(wt[None], (NZ, SHARD, GROUP)), Z_GROUPS)
    blocks = [wt, send(wt, OTHER)]

    attended, prob = call(
        forward_body,
        (shape(TOK, GROUP), shape(HEADS, TOK, TOK, dtype=F32)),
        flops=4 * 4 * TOK * TOK * HEAD,
        moved=2 << 20,
    )(doc_lengths[0], query_rows, key_rows, value_matrix)
    heads = send(attended, TURN)
    heads = [heads] + [send(heads, pairs) for pairs in ALONG_Y]

    big = 2 * 4 * TOK * COLS * GROUP
    grad_part = call(
        weight_grad_body,
        shape(COLS, GROUP),
        scratch=(pltpu.VMEM((4, TOK, GROUP), BF),),
        flops=big,
        moved=6 << 20,
    )(place, *cols, *heads)
    grad_rows = exchange(grad_part.reshape(NZ, 2 * SHARD, GROUP), Z_GROUPS)

    pair, attended_two, wt_all = call(
        layer_pair_body,
        (shape(2, TOK, COLS), shape(2, TOK, GROUP), shape(COLS, GROUP)),
        scratch=(pltpu.VMEM((4, TOK, GROUP), BF),),
        flops=big // 2,
        moved=6 << 20,
    )(place, *heads, *blocks)
    pair = send(pair, SWAP)
    across = call(
        layer_across_body, shape(TOK, COLS), flops=big // 4, moved=3 << 20
    )(place, attended_two, wt_all, pair)
    across = send(across, ACROSS)
    layer_out = call(
        layer_sum_body, shape(TOK, COLS), flops=big // 4, moved=4 << 20
    )(place, attended_two, wt_all, pair, across)

    partials = call(
        attn_grad_body,
        (shape(TOK, GROUP),) * 4,
        scratch=(pltpu.VMEM((4, TOK, COLS), BF),),
        flops=big,
        moved=6 << 20,
    )(place, *cols, wt_all)
    partials = [partials[0]] + [send(p, pairs) for p, pairs in zip(partials[1:], ALONG_Y)]
    upstream = call(sum_four_body, shape(TOK, GROUP), moved=1 << 20)(place, *partials)
    upstream = send(upstream, TURN)

    query_grad, key_grad, value_grad = call(
        backward_body,
        (shape(TOK, GROUP), shape(TOK, HEAD), shape(TOK, HEAD)),
        flops=5 * 4 * 2 * TOK * TOK * HEAD,
        moved=3 << 20,
    )(place, upstream, query_rows, key_rows, value_matrix, prob)

    pieces = call(sum_z_body, (shape(SHARD, GROUP),) * 2, moved=2 << 20)(place, grad_rows)
    pieces = [send(piece, pairs).astype(F32) for piece, pairs in zip(pieces, TO_OWNER)]
    weight_grad = pieces[0] + pieces[1]
    return (layer_out, query_grad, key_grad, value_grad, weight_grad.T)


def solution(mesh):
    placed = (
        P("dp", "mp"),
        P("dp", "mp"),
        P("dp", "mp"),
        P("mp", "dp"),
        P("dp", "mp"),
        P("dp", None),
    )
    return jax.shard_map(
        per_device,
        mesh=mesh,
        in_specs=placed,
        out_specs=(P("dp", "mp"), P("dp", "mp"), P("dp", "mp"), P("dp", "mp"), P("mp", "dp")),
        check_vma=False,
    )
```

```python
import jax
import jax.numpy as jnp
from jax import lax
from jax.experimental import pallas as pl
from jax.experimental.pallas import tpu as pltpu
from jax.sharding import PartitionSpec as P


NX, NZ, NC, NY = 4, 8, 2, 4
HEAD = 128
TOK = 256
HEADS = 4
GROUP = HEADS * HEAD
COLS = 1280
SHARD = 80
AXES = ("dp", "mp")
BF, F32 = jnp.bfloat16, jnp.float32
SCALE = HEAD ** -0.5


def route(target):
    pairs = []
    for x in range(NX):
        for z in range(NZ):
            for c in range(NC):
                for y in range(NY):
                    tx, tz, tc, ty = target(x, z, c, y)
                    src = ((x * NZ + z) * NC + c) * NY + y
                    pairs.append((src, ((tx * NZ + tz) * NC + tc) * NY + ty))
    return pairs


def low_of(x):
    return (x + x // 2) % 2


def chip(high, low):
    return 3 - low if high else low


SWAP = route(lambda x, z, c, y: (x, z, 1 - c, y))
ACROSS = route(lambda x, z, c, y: (x ^ 1, z, c, y))
OTHER = route(lambda x, z, c, y: (3 - x, z, c, y))
TO_PLANE = route(lambda x, z, c, y: (chip(c, y // 2), z, y % 2, x))
TO_OWNER = [
    route(lambda x, z, c, y, k=k: (y, z, (x // 2 + k) % 2, 2 * low_of(x) + c)) for k in range(2)
]
TURN = route(lambda x, z, c, y: (chip(x // 2, y // 2), z, y % 2, 2 * low_of(x) + c))
ALONG_Y = [route(lambda x, z, c, y, k=k: (x, z, c, (y + k) % 4)) for k in range(1, 4)]
Z_GROUPS = [[(x * NZ + z) * NC + c for z in range(NZ)] for x in range(NX) for c in range(NC)]


def send(value, pairs):
    return lax.ppermute(value, AXES, pairs)


def exchange(blocks, groups):
    return lax.all_to_all(blocks, "dp", 0, 0, axis_index_groups=groups, tiled=True)


def dot(a, b, dims):
    return lax.dot_general(a, b, (dims, ((), ())), preferred_element_type=F32)


def whole(array):
    dims = array.shape
    return pl.BlockSpec(dims, lambda i: (0,) * len(dims), pipeline_mode=pl.Buffered(1))


def call(body, outs, scratch=(), flops=0, moved=0, limit=12):
    def run(scalars, *operands):
        return pl.pallas_call(
            body,
            out_shape=outs,
            grid=(1,),
            in_specs=[pl.BlockSpec(memory_space=pltpu.SMEM)] + [whole(a) for a in operands],
            out_specs=jax.tree.map(whole, outs),
            scratch_shapes=list(scratch),
            compiler_params=pltpu.CompilerParams(vmem_limit_bytes=limit << 20),
            cost_estimate=pl.CostEstimate(flops=flops, bytes_accessed=moved, transcendentals=0),
        )(scalars, *operands)

    return run


def shape(*dims, dtype=BF):
    return jax.ShapeDtypeStruct(dims, dtype)


def forward_body(lengths, q_ref, k_ref, v_ref, att_ref, prob_ref):
    rows = lax.broadcasted_iota(jnp.int32, (TOK, TOK), 0)
    cols = lax.broadcasted_iota(jnp.int32, (TOK, TOK), 1)
    row_at = lax.broadcasted_iota(jnp.int32, (TOK, 1), 0)
    col_at = lax.broadcasted_iota(jnp.int32, (1, TOK), 1)
    row_seg = jnp.zeros((TOK, 1), jnp.int32)
    col_seg = jnp.zeros((1, TOK), jnp.int32)
    end = jnp.int32(0)
    for i in range(8):
        end = end + lengths[i]
        row_seg = row_seg + (row_at >= end).astype(jnp.int32)
        col_seg = col_seg + (col_at >= end).astype(jnp.int32)
    allowed = (row_seg == col_seg) & (rows >= cols)
    for h in range(HEADS):
        at = slice(h * HEAD, (h + 1) * HEAD)
        logits = dot(q_ref[:, at], k_ref[...], ((1,), (1,))) * SCALE
        logits = jnp.where(allowed, logits, -jnp.inf)
        terms = jnp.exp(logits - jnp.max(logits, axis=-1, keepdims=True))
        prob = terms / jnp.sum(terms, axis=-1, keepdims=True)
        prob_ref[h] = prob
        att_ref[:, at] = dot(prob.astype(BF), v_ref[...], ((1,), (0,))).astype(BF)


def sum_four_body(_, a0, a1, a2, a3, out):
    out[...] = (
        (a0[...].astype(F32) + a1[...].astype(F32)) + (a2[...].astype(F32) + a3[...].astype(F32))
    ).astype(BF)


def backward_body(_, up_ref, q_ref, k_ref, v_ref, prob_ref, dq_ref, dk_ref, dv_ref):
    key_sum = jnp.zeros((TOK, HEAD), F32)
    value_sum = jnp.zeros((TOK, HEAD), F32)
    for h in range(HEADS):
        at = slice(h * HEAD, (h + 1) * HEAD)
        up = up_ref[:, at]
        prob = prob_ref[h]
        prob_grad = dot(up, v_ref[...], ((1,), (1,)))
        delta = jnp.sum(prob * prob_grad, axis=-1, keepdims=True)
        score = (prob * (prob_grad - delta) * SCALE).astype(BF)
        dq_ref[:, at] = dot(score, k_ref[...], ((1,), (0,))).astype(BF)
        key_sum = key_sum + dot(score, q_ref[:, at], ((0,), (0,)))
        value_sum = value_sum + dot(prob.astype(BF), up, ((0,), (0,)))
    dk_ref[...] = key_sum.astype(BF)
    dv_ref[...] = value_sum.astype(BF)


def weight_grad_body(place, o0, o1, o2, o3, r0, r1, r2, r3, grad_ref, att):
    g, y = place[0], place[1]
    for k, ref in enumerate((r0, r1, r2, r3)):
        att[jnp.bitwise_xor((y + 4 - k) % 4, g)] = ref[...]
    for i in range(COLS // 256):
        at = slice(i * 256, (i + 1) * 256)
        total = dot(o0[:, at], att[0], ((0,), (0,)))
        for r, ref in ((1, o1), (2, o2), (3, o3)):
            total = total + dot(ref[:, at], att[r], ((0,), (0,)))
        grad_ref[at, :] = total.astype(BF)


def layer_pair_body(place, r0, r1, r2, r3, wt, pair_ref, att_ref, att):
    g, y = place[0], place[1]
    for k, ref in enumerate((r0, r1, r2, r3)):
        att[jnp.bitwise_xor((y + 4 - k) % 4, g)] = ref[...]
    for i in range(2):
        pair_ref[i] = dot(att[2 * i + 1], wt[...], ((1,), (1,))).astype(BF)
        att_ref[i] = att[2 * i]


def layer_across_body(_, att, wt, pair, out):
    out[...] = (dot(att[1], wt[...], ((1,), (1,))) + pair[1].astype(F32)).astype(BF)


def layer_sum_body(_, att, wt, pair, across, out):
    out[...] = (
        dot(att[0], wt[...], ((1,), (1,))) + pair[0].astype(F32) + across[...].astype(F32)
    ).astype(BF)


def attn_grad_body(place, o0, o1, o2, o3, w0, w1, g0, g1, g2, g3, wt_ref, og):
    g, y, high = place[0], place[1], place[2]
    for k, ref in enumerate((w0, w1)):
        c = (high + k) % 2
        for z in range(NZ):
            wt_ref[pl.ds(pl.multiple_of(z * 160 + c * SHARD, 16), SHARD), :] = ref[z]
    for r, ref in enumerate((o0, o1, o2, o3)):
        og[r] = ref[...]
    for k, ref in enumerate((g0, g1, g2, g3)):
        at = jnp.bitwise_xor((y + k) % 4, g)
        ref[...] = dot(og[at], wt_ref[...], ((1,), (0,))).astype(BF)


def sum_z_body(place, blocks, o0, o1):
    high = place[2]
    for k, ref in enumerate((o0, o1)):
        at = pl.ds(pl.multiple_of((high + k) % 2 * SHARD, 16), SHARD)
        total = blocks[0, at, :].astype(F32)
        for z in range(1, NZ):
            total = total + blocks[z, at, :].astype(F32)
        ref[...] = total.astype(BF)


def per_device(query_rows, key_rows, value_matrix, out_weight, out_grad, doc_lengths):
    dp, y = lax.axis_index("dp"), lax.axis_index("mp")
    x = dp // (NZ * NC)
    place = jnp.stack([2 * low_of(x) + dp % NC, y, x // 2]).astype(jnp.int32)
    across_grad = send(out_grad, ACROSS)
    cols = [out_grad, send(out_grad, SWAP), across_grad, send(across_grad, SWAP)]

    wt = send(out_weight.T, TO_PLANE)
    wt = exchange(jnp.broadcast_to(wt[None], (NZ, SHARD, GROUP)), Z_GROUPS)
    blocks = [wt, send(wt, OTHER)]

    attended, prob = call(
        forward_body,
        (shape(TOK, GROUP), shape(HEADS, TOK, TOK, dtype=F32)),
        flops=4 * 4 * TOK * TOK * HEAD,
        moved=2 << 20,
        limit=63,
    )(doc_lengths[0], query_rows, key_rows, value_matrix)
    heads = send(attended, TURN)
    heads = [heads] + [send(heads, pairs) for pairs in ALONG_Y]

    big = 2 * 4 * TOK * COLS * GROUP
    grad_part = call(
        weight_grad_body,
        shape(COLS, GROUP),
        scratch=(pltpu.VMEM((4, TOK, GROUP), BF),),
        flops=big,
        moved=6 << 20,
    )(place, *cols, *heads)
    grad_rows = exchange(grad_part.reshape(NZ, 2 * SHARD, GROUP), Z_GROUPS)

    *partials, wt_all = call(
        attn_grad_body,
        (shape(TOK, GROUP),) * 4 + (shape(COLS, GROUP),),
        scratch=(pltpu.VMEM((4, TOK, COLS), BF),),
        flops=big,
        moved=6 << 20,
    )(place, *cols, *blocks)

    pair, attended_two = call(
        layer_pair_body,
        (shape(2, TOK, COLS), shape(2, TOK, GROUP)),
        scratch=(pltpu.VMEM((4, TOK, GROUP), BF),),
        flops=big // 2,
        moved=4 << 20,
    )(place, *heads, wt_all)
    pair = send(pair, SWAP)
    across = call(
        layer_across_body, shape(TOK, COLS), flops=big // 4, moved=3 << 20
    )(place, attended_two, wt_all, pair)
    across = send(across, ACROSS)
    layer_out = call(
        layer_sum_body, shape(TOK, COLS), flops=big // 4, moved=4 << 20
    )(place, attended_two, wt_all, pair, across)

    partials = [partials[0]] + [send(p, pairs) for p, pairs in zip(partials[1:], ALONG_Y)]
    upstream = call(sum_four_body, shape(TOK, GROUP), moved=1 << 20)(place, *partials)
    upstream = send(upstream, TURN)

    query_grad, key_grad, value_grad = call(
        backward_body,
        (shape(TOK, GROUP), shape(TOK, HEAD), shape(TOK, HEAD)),
        flops=5 * 4 * 2 * TOK * TOK * HEAD,
        moved=3 << 20,
    )(place, upstream, query_rows, key_rows, value_matrix, prob)

    pieces = call(sum_z_body, (shape(SHARD, GROUP),) * 2, moved=2 << 20)(place, grad_rows)
    pieces = [send(piece, pairs).astype(F32) for piece, pairs in zip(pieces, TO_OWNER)]
    weight_grad = pieces[0] + pieces[1]
    return (layer_out, query_grad, key_grad, value_grad, weight_grad.T)


def solution(mesh):
    placed = (
        P("dp", "mp"),
        P("dp", "mp"),
        P("dp", "mp"),
        P("mp", "dp"),
        P("dp", "mp"),
        P("dp", None),
    )
    return jax.shard_map(
        per_device,
        mesh=mesh,
        in_specs=placed,
        out_specs=(P("dp", "mp"), P("dp", "mp"), P("dp", "mp"), P("dp", "mp"), P("mp", "dp")),
        check_vma=False,
    )
```

```python
import jax
import jax.numpy as jnp
from jax import lax
from jax.experimental import pallas as pl
from jax.experimental.pallas import tpu as pltpu
from jax.sharding import PartitionSpec as P


NX, NZ, NC, NY = 4, 8, 2, 4
HEAD = 128
TOK = 256
HEADS = 4
GROUP = HEADS * HEAD
COLS = 1280
SHARD = 80
AXES = ("dp", "mp")
BF, F32 = jnp.bfloat16, jnp.float32
SCALE = HEAD ** -0.5


def route(target):
    pairs = []
    for x in range(NX):
        for z in range(NZ):
            for c in range(NC):
                for y in range(NY):
                    tx, tz, tc, ty = target(x, z, c, y)
                    src = ((x * NZ + z) * NC + c) * NY + y
                    pairs.append((src, ((tx * NZ + tz) * NC + tc) * NY + ty))
    return pairs


def low_of(x):
    return (x + x // 2) % 2


def chip(high, low):
    return 3 - low if high else low


SWAP = route(lambda x, z, c, y: (x, z, 1 - c, y))
ACROSS = route(lambda x, z, c, y: (x ^ 1, z, c, y))
OTHER = route(lambda x, z, c, y: (3 - x, z, c, y))
TO_PLANE = route(lambda x, z, c, y: (chip(c, y // 2), z, y % 2, x))
TO_OWNER = [
    route(lambda x, z, c, y, k=k: (y, z, (x // 2 + k) % 2, 2 * low_of(x) + c)) for k in range(2)
]
TURN = route(lambda x, z, c, y: (chip(x // 2, y // 2), z, y % 2, 2 * low_of(x) + c))
ALONG_Y = [route(lambda x, z, c, y, k=k: (x, z, c, (y + k) % 4)) for k in range(1, 4)]
Z_GROUPS = [[(x * NZ + z) * NC + c for z in range(NZ)] for x in range(NX) for c in range(NC)]


def send(value, pairs):
    return lax.ppermute(value, AXES, pairs)


def exchange(blocks, groups):
    return lax.all_to_all(blocks, "dp", 0, 0, axis_index_groups=groups, tiled=True)


def dot(a, b, dims):
    return lax.dot_general(a, b, (dims, ((), ())), preferred_element_type=F32)


def whole(array):
    dims = array.shape
    return pl.BlockSpec(dims, lambda i: (0,) * len(dims), pipeline_mode=pl.Buffered(1))


def call(body, outs, scratch=(), flops=0, moved=0, limit=12):
    def run(scalars, *operands):
        return pl.pallas_call(
            body,
            out_shape=outs,
            grid=(1,),
            in_specs=[pl.BlockSpec(memory_space=pltpu.SMEM)] + [whole(a) for a in operands],
            out_specs=jax.tree.map(whole, outs),
            scratch_shapes=list(scratch),
            compiler_params=pltpu.CompilerParams(vmem_limit_bytes=limit << 20),
            cost_estimate=pl.CostEstimate(flops=flops, bytes_accessed=moved, transcendentals=0),
        )(scalars, *operands)

    return run


def shape(*dims, dtype=BF):
    return jax.ShapeDtypeStruct(dims, dtype)


def forward_body(lengths, q_ref, k_ref, v_ref, att_ref, prob_ref):
    rows = lax.broadcasted_iota(jnp.int32, (TOK, TOK), 0)
    cols = lax.broadcasted_iota(jnp.int32, (TOK, TOK), 1)
    row_at = lax.broadcasted_iota(jnp.int32, (TOK, 1), 0)
    col_at = lax.broadcasted_iota(jnp.int32, (1, TOK), 1)
    row_seg = jnp.zeros((TOK, 1), jnp.int32)
    col_seg = jnp.zeros((1, TOK), jnp.int32)
    end = jnp.int32(0)
    for i in range(8):
        end = end + lengths[i]
        row_seg = row_seg + (row_at >= end).astype(jnp.int32)
        col_seg = col_seg + (col_at >= end).astype(jnp.int32)
    allowed = (row_seg == col_seg) & (rows >= cols)
    for h in range(HEADS):
        at = slice(h * HEAD, (h + 1) * HEAD)
        logits = dot(q_ref[:, at], k_ref[...], ((1,), (1,))) * SCALE
        logits = jnp.where(allowed, logits, -jnp.inf)
        terms = jnp.exp(logits - jnp.max(logits, axis=-1, keepdims=True))
        prob = terms / jnp.sum(terms, axis=-1, keepdims=True)
        prob_ref[h] = prob
        att_ref[:, at] = dot(prob.astype(BF), v_ref[...], ((1,), (0,))).astype(BF)


def sum_four_body(_, a0, a1, a2, a3, out):
    out[...] = (
        (a0[...].astype(F32) + a1[...].astype(F32)) + (a2[...].astype(F32) + a3[...].astype(F32))
    ).astype(BF)


def backward_body(_, up_ref, q_ref, k_ref, v_ref, prob_ref, dq_ref, dk_ref, dv_ref):
    key_sum = jnp.zeros((TOK, HEAD), F32)
    value_sum = jnp.zeros((TOK, HEAD), F32)
    for h in range(HEADS):
        at = slice(h * HEAD, (h + 1) * HEAD)
        up = up_ref[:, at]
        prob = prob_ref[h]
        prob_grad = dot(up, v_ref[...], ((1,), (1,)))
        delta = jnp.sum(prob * prob_grad, axis=-1, keepdims=True)
        score = (prob * (prob_grad - delta) * SCALE).astype(BF)
        dq_ref[:, at] = dot(score, k_ref[...], ((1,), (0,))).astype(BF)
        key_sum = key_sum + dot(score, q_ref[:, at], ((0,), (0,)))
        value_sum = value_sum + dot(prob.astype(BF), up, ((0,), (0,)))
    dk_ref[...] = key_sum.astype(BF)
    dv_ref[...] = value_sum.astype(BF)


def weight_grad_body(place, o0, o1, o2, o3, r0, r1, r2, r3, grad_ref, att):
    g, y = place[0], place[1]
    for k, ref in enumerate((r0, r1, r2, r3)):
        att[jnp.bitwise_xor((y + 4 - k) % 4, g)] = ref[...]
    for i in range(COLS // 256):
        at = slice(i * 256, (i + 1) * 256)
        total = dot(o0[:, at], att[0], ((0,), (0,)))
        for r, ref in ((1, o1), (2, o2), (3, o3)):
            total = total + dot(ref[:, at], att[r], ((0,), (0,)))
        grad_ref[at, :] = total.astype(BF)


def layer_pair_body(place, r0, r1, r2, r3, wt, pair_ref, att_ref, att):
    g, y = place[0], place[1]
    for k, ref in enumerate((r0, r1, r2, r3)):
        att[jnp.bitwise_xor((y + 4 - k) % 4, g)] = ref[...]
    for i in range(2):
        pair_ref[i] = dot(att[2 * i + 1], wt[...], ((1,), (1,))).astype(BF)
        att_ref[i] = att[2 * i]


def layer_across_body(_, att, wt, pair, out):
    out[...] = (dot(att[1], wt[...], ((1,), (1,))) + pair[1].astype(F32)).astype(BF)


def layer_own_body(_, att, wt, pair, out):
    out[...] = (dot(att[0], wt[...], ((1,), (1,))) + pair[0].astype(F32)).astype(BF)


def attn_grad_body(place, o0, o1, o2, o3, w0, w1, g0, g1, g2, g3, wt_ref, og):
    g, y, high = place[0], place[1], place[2]
    for k, ref in enumerate((w0, w1)):
        c = (high + k) % 2
        for z in range(NZ):
            wt_ref[pl.ds(pl.multiple_of(z * 160 + c * SHARD, 16), SHARD), :] = ref[z]
    for r, ref in enumerate((o0, o1, o2, o3)):
        og[r] = ref[...]
    for k, ref in enumerate((g0, g1, g2, g3)):
        at = jnp.bitwise_xor((y + k) % 4, g)
        ref[...] = dot(og[at], wt_ref[...], ((1,), (0,))).astype(BF)


def sum_z_body(place, blocks, o0, o1):
    high = place[2]
    for k, ref in enumerate((o0, o1)):
        at = pl.ds(pl.multiple_of((high + k) % 2 * SHARD, 16), SHARD)
        total = blocks[0, at, :].astype(F32)
        for z in range(1, NZ):
            total = total + blocks[z, at, :].astype(F32)
        ref[...] = total.astype(BF)


def per_device(query_rows, key_rows, value_matrix, out_weight, out_grad, doc_lengths):
    dp, y = lax.axis_index("dp"), lax.axis_index("mp")
    x = dp // (NZ * NC)
    place = jnp.stack([2 * low_of(x) + dp % NC, y, x // 2]).astype(jnp.int32)
    across_grad = send(out_grad, ACROSS)
    cols = [out_grad, send(out_grad, SWAP), across_grad, send(across_grad, SWAP)]

    wt = send(out_weight.T, TO_PLANE)
    wt = exchange(jnp.broadcast_to(wt[None], (NZ, SHARD, GROUP)), Z_GROUPS)
    blocks = [wt, send(wt, OTHER)]

    attended, prob = call(
        forward_body,
        (shape(TOK, GROUP), shape(HEADS, TOK, TOK, dtype=F32)),
        flops=4 * 4 * TOK * TOK * HEAD,
        moved=2 << 20,
        limit=63,
    )(doc_lengths[0], query_rows, key_rows, value_matrix)
    heads = send(attended, TURN)
    heads = [heads] + [send(heads, pairs) for pairs in ALONG_Y]

    big = 2 * 4 * TOK * COLS * GROUP
    grad_part = call(
        weight_grad_body,
        shape(COLS, GROUP),
        scratch=(pltpu.VMEM((4, TOK, GROUP), BF),),
        flops=big,
        moved=6 << 20,
    )(place, *cols, *heads)
    grad_rows = exchange(grad_part.reshape(NZ, 2 * SHARD, GROUP), Z_GROUPS)

    *partials, wt_all = call(
        attn_grad_body,
        (shape(TOK, GROUP),) * 4 + (shape(COLS, GROUP),),
        scratch=(pltpu.VMEM((4, TOK, COLS), BF),),
        flops=big,
        moved=6 << 20,
    )(place, *cols, *blocks)

    pair, attended_two = call(
        layer_pair_body,
        (shape(2, TOK, COLS), shape(2, TOK, GROUP)),
        scratch=(pltpu.VMEM((4, TOK, GROUP), BF),),
        flops=big // 2,
        moved=4 << 20,
    )(place, *heads, wt_all)
    pair = send(pair, SWAP)
    across = call(
        layer_across_body, shape(TOK, COLS), flops=big // 4, moved=3 << 20
    )(place, attended_two, wt_all, pair)
    across = send(across, ACROSS)
    own = call(layer_own_body, shape(TOK, COLS), flops=big // 4, moved=4 << 20)(
        place, attended_two, wt_all, pair
    )
    layer_out = (own.astype(F32) + across.astype(F32)).astype(BF)

    partials = [partials[0]] + [send(p, pairs) for p, pairs in zip(partials[1:], ALONG_Y)]
    upstream = call(sum_four_body, shape(TOK, GROUP), moved=1 << 20)(place, *partials)
    upstream = send(upstream, TURN)

    query_grad, key_grad, value_grad = call(
        backward_body,
        (shape(TOK, GROUP), shape(TOK, HEAD), shape(TOK, HEAD)),
        flops=5 * 4 * 2 * TOK * TOK * HEAD,
        moved=3 << 20,
    )(place, upstream, query_rows, key_rows, value_matrix, prob)

    pieces = call(sum_z_body, (shape(SHARD, GROUP),) * 2, moved=2 << 20)(place, grad_rows)
    pieces = [send(piece, pairs).astype(F32) for piece, pairs in zip(pieces, TO_OWNER)]
    weight_grad = pieces[0] + pieces[1]
    return (layer_out, query_grad, key_grad, value_grad, weight_grad.T)


def solution(mesh):
    placed = (
        P("dp", "mp"),
        P("dp", "mp"),
        P("dp", "mp"),
        P("mp", "dp"),
        P("dp", "mp"),
        P("dp", None),
    )
    return jax.shard_map(
        per_device,
        mesh=mesh,
        in_specs=placed,
        out_specs=(P("dp", "mp"), P("dp", "mp"), P("dp", "mp"), P("dp", "mp"), P("mp", "dp")),
        check_vma=False,
    )
```

```python
import jax
import jax.numpy as jnp
from jax import lax
from jax.experimental import pallas as pl
from jax.experimental.pallas import tpu as pltpu
from jax.sharding import PartitionSpec as P


NX, NZ, NC, NY = 4, 8, 2, 4
HEAD = 128
TOK = 256
HEADS = 4
GROUP = HEADS * HEAD
COLS = 1280
SHARD = 80
AXES = ("dp", "mp")
BF, F32 = jnp.bfloat16, jnp.float32
SCALE = HEAD ** -0.5


def route(target):
    pairs = []
    for x in range(NX):
        for z in range(NZ):
            for c in range(NC):
                for y in range(NY):
                    tx, tz, tc, ty = target(x, z, c, y)
                    src = ((x * NZ + z) * NC + c) * NY + y
                    pairs.append((src, ((tx * NZ + tz) * NC + tc) * NY + ty))
    return pairs


def low_of(x):
    return (x + x // 2) % 2


def chip(high, low):
    return 3 - low if high else low


SWAP = route(lambda x, z, c, y: (x, z, 1 - c, y))
ACROSS = route(lambda x, z, c, y: (x ^ 1, z, c, y))
OTHER = route(lambda x, z, c, y: (3 - x, z, c, y))
TO_PLANE = route(lambda x, z, c, y: (chip(c, y // 2), z, y % 2, x))
TO_OWNER = [
    route(lambda x, z, c, y, k=k: (y, z, (x // 2 + k) % 2, 2 * low_of(x) + c)) for k in range(2)
]
TURN = route(lambda x, z, c, y: (chip(x // 2, y // 2), z, y % 2, 2 * low_of(x) + c))
ALONG_Y = [route(lambda x, z, c, y, k=k: (x, z, c, (y + k) % 4)) for k in range(1, 4)]
Z_GROUPS = [[(x * NZ + z) * NC + c for z in range(NZ)] for x in range(NX) for c in range(NC)]


def send(value, pairs):
    return lax.ppermute(value, AXES, pairs)


def exchange(blocks, groups):
    return lax.all_to_all(blocks, "dp", 0, 0, axis_index_groups=groups, tiled=True)


def dot(a, b, dims):
    return lax.dot_general(a, b, (dims, ((), ())), preferred_element_type=F32)


def whole(array):
    dims = array.shape
    return pl.BlockSpec(dims, lambda i: (0,) * len(dims), pipeline_mode=pl.Buffered(1))


def call(body, outs, scratch=(), flops=0, moved=0, limit=12):
    def run(scalars, *operands):
        return pl.pallas_call(
            body,
            out_shape=outs,
            grid=(1,),
            in_specs=[pl.BlockSpec(memory_space=pltpu.SMEM)] + [whole(a) for a in operands],
            out_specs=jax.tree.map(whole, outs),
            scratch_shapes=list(scratch),
            compiler_params=pltpu.CompilerParams(vmem_limit_bytes=limit << 20),
            cost_estimate=pl.CostEstimate(flops=flops, bytes_accessed=moved, transcendentals=0),
        )(scalars, *operands)

    return run


def shape(*dims, dtype=BF):
    return jax.ShapeDtypeStruct(dims, dtype)


def forward_body(lengths, q_ref, k_ref, v_ref, att_ref, prob_ref):
    rows = lax.broadcasted_iota(jnp.int32, (TOK, TOK), 0)
    cols = lax.broadcasted_iota(jnp.int32, (TOK, TOK), 1)
    row_at = lax.broadcasted_iota(jnp.int32, (TOK, 1), 0)
    col_at = lax.broadcasted_iota(jnp.int32, (1, TOK), 1)
    row_seg = jnp.zeros((TOK, 1), jnp.int32)
    col_seg = jnp.zeros((1, TOK), jnp.int32)
    end = jnp.int32(0)
    for i in range(8):
        end = end + lengths[i]
        row_seg = row_seg + (row_at >= end).astype(jnp.int32)
        col_seg = col_seg + (col_at >= end).astype(jnp.int32)
    allowed = (row_seg == col_seg) & (rows >= cols)
    for h in range(HEADS):
        at = slice(h * HEAD, (h + 1) * HEAD)
        logits = dot(q_ref[:, at], k_ref[...], ((1,), (1,))) * SCALE
        logits = jnp.where(allowed, logits, -jnp.inf)
        terms = jnp.exp(logits - jnp.max(logits, axis=-1, keepdims=True))
        prob = terms / jnp.sum(terms, axis=-1, keepdims=True)
        prob_ref[h] = prob
        att_ref[:, at] = dot(prob.astype(BF), v_ref[...], ((1,), (0,))).astype(BF)


def sum_four_body(_, a0, a1, a2, a3, out):
    out[...] = (
        (a0[...].astype(F32) + a1[...].astype(F32)) + (a2[...].astype(F32) + a3[...].astype(F32))
    ).astype(BF)


def backward_body(_, up_ref, q_ref, k_ref, v_ref, prob_ref, own, across, dq_ref, dk_ref, dv_ref, out):
    out[...] = (own[...].astype(F32) + across[...].astype(F32)).astype(BF)
    key_sum = jnp.zeros((TOK, HEAD), F32)
    value_sum = jnp.zeros((TOK, HEAD), F32)
    for h in range(HEADS):
        at = slice(h * HEAD, (h + 1) * HEAD)
        up = up_ref[:, at]
        prob = prob_ref[h]
        prob_grad = dot(up, v_ref[...], ((1,), (1,)))
        delta = jnp.sum(prob * prob_grad, axis=-1, keepdims=True)
        score = (prob * (prob_grad - delta) * SCALE).astype(BF)
        dq_ref[:, at] = dot(score, k_ref[...], ((1,), (0,))).astype(BF)
        key_sum = key_sum + dot(score, q_ref[:, at], ((0,), (0,)))
        value_sum = value_sum + dot(prob.astype(BF), up, ((0,), (0,)))
    dk_ref[...] = key_sum.astype(BF)
    dv_ref[...] = value_sum.astype(BF)


def weight_grad_body(place, o0, o1, o2, o3, r0, r1, r2, r3, grad_ref, att):
    g, y = place[0], place[1]
    for k, ref in enumerate((r0, r1, r2, r3)):
        att[jnp.bitwise_xor((y + 4 - k) % 4, g)] = ref[...]
    for i in range(COLS // 256):
        at = slice(i * 256, (i + 1) * 256)
        total = dot(o0[:, at], att[0], ((0,), (0,)))
        for r, ref in ((1, o1), (2, o2), (3, o3)):
            total = total + dot(ref[:, at], att[r], ((0,), (0,)))
        grad_ref[at, :] = total.astype(BF)


def layer_pair_body(place, r0, r1, r2, r3, wt, pair_ref, att_ref, att):
    g, y = place[0], place[1]
    for k, ref in enumerate((r0, r1, r2, r3)):
        att[jnp.bitwise_xor((y + 4 - k) % 4, g)] = ref[...]
    for i in range(2):
        pair_ref[i] = dot(att[2 * i + 1], wt[...], ((1,), (1,))).astype(BF)
        att_ref[i] = att[2 * i]


def layer_across_body(_, att, wt, pair, out):
    out[...] = (dot(att[1], wt[...], ((1,), (1,))) + pair[1].astype(F32)).astype(BF)


def layer_own_body(_, att, wt, pair, out):
    out[...] = (dot(att[0], wt[...], ((1,), (1,))) + pair[0].astype(F32)).astype(BF)


def attn_grad_body(place, o0, o1, o2, o3, w0, w1, g0, g1, g2, g3, wt_ref, og):
    g, y, high = place[0], place[1], place[2]
    for k, ref in enumerate((w0, w1)):
        c = (high + k) % 2
        for z in range(NZ):
            wt_ref[pl.ds(pl.multiple_of(z * 160 + c * SHARD, 16), SHARD), :] = ref[z]
    for r, ref in enumerate((o0, o1, o2, o3)):
        og[r] = ref[...]
    for k, ref in enumerate((g0, g1, g2, g3)):
        at = jnp.bitwise_xor((y + k) % 4, g)
        ref[...] = dot(og[at], wt_ref[...], ((1,), (0,))).astype(BF)


def sum_z_body(place, blocks, o0, o1):
    high = place[2]
    for k, ref in enumerate((o0, o1)):
        at = pl.ds(pl.multiple_of((high + k) % 2 * SHARD, 16), SHARD)
        total = blocks[0, at, :].astype(F32)
        for z in range(1, NZ):
            total = total + blocks[z, at, :].astype(F32)
        ref[...] = total.astype(BF)


def per_device(query_rows, key_rows, value_matrix, out_weight, out_grad, doc_lengths):
    dp, y = lax.axis_index("dp"), lax.axis_index("mp")
    x = dp // (NZ * NC)
    place = jnp.stack([2 * low_of(x) + dp % NC, y, x // 2]).astype(jnp.int32)
    across_grad = send(out_grad, ACROSS)
    cols = [out_grad, send(out_grad, SWAP), across_grad, send(across_grad, SWAP)]

    wt = send(out_weight.T, TO_PLANE)
    wt = exchange(jnp.broadcast_to(wt[None], (NZ, SHARD, GROUP)), Z_GROUPS)
    blocks = [wt, send(wt, OTHER)]

    attended, prob = call(
        forward_body,
        (shape(TOK, GROUP), shape(HEADS, TOK, TOK, dtype=F32)),
        flops=4 * 4 * TOK * TOK * HEAD,
        moved=2 << 20,
        limit=63,
    )(doc_lengths[0], query_rows, key_rows, value_matrix)
    heads = send(attended, TURN)
    heads = [heads] + [send(heads, pairs) for pairs in ALONG_Y]

    big = 2 * 4 * TOK * COLS * GROUP
    grad_part = call(
        weight_grad_body,
        shape(COLS, GROUP),
        scratch=(pltpu.VMEM((4, TOK, GROUP), BF),),
        flops=big,
        moved=6 << 20,
        limit=63,
    )(place, *cols, *heads)
    grad_rows = exchange(grad_part.reshape(NZ, 2 * SHARD, GROUP), Z_GROUPS)

    *partials, wt_all = call(
        attn_grad_body,
        (shape(TOK, GROUP),) * 4 + (shape(COLS, GROUP),),
        scratch=(pltpu.VMEM((4, TOK, COLS), BF),),
        flops=big,
        moved=6 << 20,
    )(place, *cols, *blocks)

    pair, attended_two = call(
        layer_pair_body,
        (shape(2, TOK, COLS), shape(2, TOK, GROUP)),
        scratch=(pltpu.VMEM((4, TOK, GROUP), BF),),
        flops=big // 2,
        moved=4 << 20,
    )(place, *heads, wt_all)
    pair = send(pair, SWAP)
    across = call(
        layer_across_body, shape(TOK, COLS), flops=big // 4, moved=3 << 20
    )(place, attended_two, wt_all, pair)
    across = send(across, ACROSS)
    own = call(layer_own_body, shape(TOK, COLS), flops=big // 4, moved=4 << 20)(
        place, attended_two, wt_all, pair
    )

    partials = [partials[0]] + [send(p, pairs) for p, pairs in zip(partials[1:], ALONG_Y)]
    upstream = call(sum_four_body, shape(TOK, GROUP), moved=1 << 20)(place, *partials)
    upstream = send(upstream, TURN)

    query_grad, key_grad, value_grad, layer_out = call(
        backward_body,
        (shape(TOK, GROUP), shape(TOK, HEAD), shape(TOK, HEAD), shape(TOK, COLS)),
        flops=5 * 4 * 2 * TOK * TOK * HEAD,
        moved=3 << 20,
        limit=63,
    )(place, upstream, query_rows, key_rows, value_matrix, prob, own, across)

    pieces = call(sum_z_body, (shape(SHARD, GROUP),) * 2, moved=2 << 20)(place, grad_rows)
    pieces = [send(piece, pairs).astype(F32) for piece, pairs in zip(pieces, TO_OWNER)]
    weight_grad = pieces[0] + pieces[1]
    return (layer_out, query_grad, key_grad, value_grad, weight_grad.T)


def solution(mesh):
    placed = (
        P("dp", "mp"),
        P("dp", "mp"),
        P("dp", "mp"),
        P("mp", "dp"),
        P("dp", "mp"),
        P("dp", None),
    )
    return jax.shard_map(
        per_device,
        mesh=mesh,
        in_specs=placed,
        out_specs=(P("dp", "mp"), P("dp", "mp"), P("dp", "mp"), P("dp", "mp"), P("mp", "dp")),
        check_vma=False,
    )
```

```python
import jax
import jax.numpy as jnp
from jax import lax
from jax.experimental import pallas as pl
from jax.experimental.pallas import tpu as pltpu
from jax.sharding import PartitionSpec as P


NX, NZ, NC, NY = 4, 8, 2, 4
HEAD = 128
TOK = 256
HEADS = 4
GROUP = HEADS * HEAD
COLS = 1280
SHARD = 80
AXES = ("dp", "mp")
BF, F32 = jnp.bfloat16, jnp.float32
SCALE = HEAD ** -0.5


def route(target):
    pairs = []
    for x in range(NX):
        for z in range(NZ):
            for c in range(NC):
                for y in range(NY):
                    tx, tz, tc, ty = target(x, z, c, y)
                    src = ((x * NZ + z) * NC + c) * NY + y
                    pairs.append((src, ((tx * NZ + tz) * NC + tc) * NY + ty))
    return pairs


def low_of(x):
    return (x + x // 2) % 2


def chip(high, low):
    return 3 - low if high else low


SWAP = route(lambda x, z, c, y: (x, z, 1 - c, y))
ACROSS = route(lambda x, z, c, y: (x ^ 1, z, c, y))
OTHER = route(lambda x, z, c, y: (3 - x, z, c, y))
TO_PLANE = route(lambda x, z, c, y: (chip(c, y // 2), z, y % 2, x))
TO_OWNER = [
    route(lambda x, z, c, y, k=k: (y, z, (x // 2 + k) % 2, 2 * low_of(x) + c)) for k in range(2)
]
TURN = route(lambda x, z, c, y: (chip(x // 2, y // 2), z, y % 2, 2 * low_of(x) + c))
ALONG_Y = [route(lambda x, z, c, y, k=k: (x, z, c, (y + k) % 4)) for k in range(1, 4)]
Z_GROUPS = [[(x * NZ + z) * NC + c for z in range(NZ)] for x in range(NX) for c in range(NC)]


def send(value, pairs):
    return lax.ppermute(value, AXES, pairs)


def exchange(blocks, groups):
    return lax.all_to_all(blocks, "dp", 0, 0, axis_index_groups=groups, tiled=True)


def dot(a, b, dims):
    return lax.dot_general(a, b, (dims, ((), ())), preferred_element_type=F32)


def whole(array):
    dims = array.shape
    return pl.BlockSpec(dims, lambda i: (0,) * len(dims), pipeline_mode=pl.Buffered(1))


def call(body, outs, scratch=(), flops=0, moved=0, limit=12):
    def run(scalars, *operands):
        return pl.pallas_call(
            body,
            out_shape=outs,
            grid=(1,),
            in_specs=[pl.BlockSpec(memory_space=pltpu.SMEM)] + [whole(a) for a in operands],
            out_specs=jax.tree.map(whole, outs),
            scratch_shapes=list(scratch),
            compiler_params=pltpu.CompilerParams(vmem_limit_bytes=limit << 20),
            cost_estimate=pl.CostEstimate(flops=flops, bytes_accessed=moved, transcendentals=0),
        )(scalars, *operands)

    return run


def shape(*dims, dtype=BF):
    return jax.ShapeDtypeStruct(dims, dtype)


def forward_body(place, q_ref, k_ref, v_ref, att_ref, prob_ref):
    rows = lax.broadcasted_iota(jnp.int32, (TOK, TOK), 0)
    cols = lax.broadcasted_iota(jnp.int32, (TOK, TOK), 1)
    row_at = lax.broadcasted_iota(jnp.int32, (TOK, 1), 0)
    col_at = lax.broadcasted_iota(jnp.int32, (1, TOK), 1)
    row_seg = jnp.zeros((TOK, 1), jnp.int32)
    col_seg = jnp.zeros((1, TOK), jnp.int32)
    end = jnp.int32(0)
    for i in range(8):
        end = end + place[3 + i]
        row_seg = row_seg + (row_at >= end).astype(jnp.int32)
        col_seg = col_seg + (col_at >= end).astype(jnp.int32)
    allowed = (row_seg == col_seg) & (rows >= cols)
    for h in range(HEADS):
        at = slice(h * HEAD, (h + 1) * HEAD)
        logits = dot(q_ref[:, at], k_ref[...], ((1,), (1,))) * SCALE
        logits = jnp.where(allowed, logits, -jnp.inf)
        terms = jnp.exp(logits - jnp.max(logits, axis=-1, keepdims=True))
        prob = terms / jnp.sum(terms, axis=-1, keepdims=True)
        prob_ref[h] = prob
        att_ref[:, at] = dot(prob.astype(BF), v_ref[...], ((1,), (0,))).astype(BF)


def sum_four_body(_, a0, a1, a2, a3, out):
    out[...] = (
        (a0[...].astype(F32) + a1[...].astype(F32)) + (a2[...].astype(F32) + a3[...].astype(F32))
    ).astype(BF)


def backward_body(_, up_ref, q_ref, k_ref, v_ref, prob_ref, dq_ref, dk_ref, dv_ref):
    key_sum = jnp.zeros((TOK, HEAD), F32)
    value_sum = jnp.zeros((TOK, HEAD), F32)
    for h in range(HEADS):
        at = slice(h * HEAD, (h + 1) * HEAD)
        up = up_ref[:, at]
        prob = prob_ref[h]
        prob_grad = dot(up, v_ref[...], ((1,), (1,)))
        delta = jnp.sum(prob * prob_grad, axis=-1, keepdims=True)
        score = (prob * (prob_grad - delta) * SCALE).astype(BF)
        dq_ref[:, at] = dot(score, k_ref[...], ((1,), (0,))).astype(BF)
        key_sum = key_sum + dot(score, q_ref[:, at], ((0,), (0,)))
        value_sum = value_sum + dot(prob.astype(BF), up, ((0,), (0,)))
    dk_ref[...] = key_sum.astype(BF)
    dv_ref[...] = value_sum.astype(BF)


def weight_grad_body(place, o0, o1, o2, o3, r0, r1, r2, r3, grad_ref, att):
    g, y = place[0], place[1]
    for k, ref in enumerate((r0, r1, r2, r3)):
        att[jnp.bitwise_xor((y + 4 - k) % 4, g)] = ref[...]
    for i in range(COLS // 256):
        at = slice(i * 256, (i + 1) * 256)
        total = dot(o0[:, at], att[0], ((0,), (0,)))
        for r, ref in ((1, o1), (2, o2), (3, o3)):
            total = total + dot(ref[:, at], att[r], ((0,), (0,)))
        grad_ref[at, :] = total.astype(BF)


def layer_pair_body(place, r0, r1, r2, r3, wt, pair_ref, att_ref, att):
    g, y = place[0], place[1]
    for k, ref in enumerate((r0, r1, r2, r3)):
        att[jnp.bitwise_xor((y + 4 - k) % 4, g)] = ref[...]
    for i in range(2):
        pair_ref[i] = dot(att[2 * i + 1], wt[...], ((1,), (1,))).astype(BF)
        att_ref[i] = att[2 * i]


def layer_across_body(_, att, wt, pair, out):
    out[...] = (dot(att[1], wt[...], ((1,), (1,))) + pair[1].astype(F32)).astype(BF)


def layer_own_body(_, att, wt, pair, out):
    out[...] = (dot(att[0], wt[...], ((1,), (1,))) + pair[0].astype(F32)).astype(BF)


def attn_grad_body(place, o0, o1, o2, o3, w0, w1, g0, g1, g2, g3, wt_ref, og):
    g, y, high = place[0], place[1], place[2]
    for k, ref in enumerate((w0, w1)):
        c = (high + k) % 2
        for z in range(NZ):
            wt_ref[pl.ds(pl.multiple_of(z * 160 + c * SHARD, 16), SHARD), :] = ref[z]
    for r, ref in enumerate((o0, o1, o2, o3)):
        og[r] = ref[...]
    for k, ref in enumerate((g0, g1, g2, g3)):
        at = jnp.bitwise_xor((y + k) % 4, g)
        ref[...] = dot(og[at], wt_ref[...], ((1,), (0,))).astype(BF)


def sum_z_body(place, blocks, o0, o1):
    high = place[2]
    for k, ref in enumerate((o0, o1)):
        at = pl.ds(pl.multiple_of((high + k) % 2 * SHARD, 16), SHARD)
        total = blocks[0, at, :].astype(F32)
        for z in range(1, NZ):
            total = total + blocks[z, at, :].astype(F32)
        ref[...] = total.astype(BF)


def per_device(query_rows, key_rows, value_matrix, out_weight, out_grad, doc_lengths):
    dp, y = lax.axis_index("dp"), lax.axis_index("mp")
    x = dp // (NZ * NC)
    place = jnp.stack([2 * low_of(x) + dp % NC, y, x // 2]).astype(jnp.int32)
    place = jnp.concatenate([place, doc_lengths[0]])
    across_grad = send(out_grad, ACROSS)
    cols = [out_grad, send(out_grad, SWAP), across_grad, send(across_grad, SWAP)]

    wt = send(out_weight.T, TO_PLANE)
    wt = exchange(jnp.broadcast_to(wt[None], (NZ, SHARD, GROUP)), Z_GROUPS)
    blocks = [wt, send(wt, OTHER)]

    attended, prob = call(
        forward_body,
        (shape(TOK, GROUP), shape(HEADS, TOK, TOK, dtype=F32)),
        flops=4 * 4 * TOK * TOK * HEAD,
        moved=2 << 20,
        limit=63,
    )(place, query_rows, key_rows, value_matrix)
    heads = send(attended, TURN)
    heads = [heads] + [send(heads, pairs) for pairs in ALONG_Y]

    big = 2 * 4 * TOK * COLS * GROUP
    grad_part = call(
        weight_grad_body,
        shape(COLS, GROUP),
        scratch=(pltpu.VMEM((4, TOK, GROUP), BF),),
        flops=big,
        moved=6 << 20,
    )(place, *cols, *heads)
    grad_rows = exchange(grad_part.reshape(NZ, 2 * SHARD, GROUP), Z_GROUPS)

    *partials, wt_all = call(
        attn_grad_body,
        (shape(TOK, GROUP),) * 4 + (shape(COLS, GROUP),),
        scratch=(pltpu.VMEM((4, TOK, COLS), BF),),
        flops=big,
        moved=6 << 20,
        limit=63,
    )(place, *cols, *blocks)

    pair, attended_two = call(
        layer_pair_body,
        (shape(2, TOK, COLS), shape(2, TOK, GROUP)),
        scratch=(pltpu.VMEM((4, TOK, GROUP), BF),),
        flops=big // 2,
        moved=4 << 20,
    )(place, *heads, wt_all)
    pair = send(pair, SWAP)
    across = call(
        layer_across_body, shape(TOK, COLS), flops=big // 4, moved=3 << 20
    )(place, attended_two, wt_all, pair)
    across = send(across, ACROSS)
    own = call(layer_own_body, shape(TOK, COLS), flops=big // 4, moved=4 << 20)(
        place, attended_two, wt_all, pair
    )
    layer_out = (own.astype(F32) + across.astype(F32)).astype(BF)

    partials = [partials[0]] + [send(p, pairs) for p, pairs in zip(partials[1:], ALONG_Y)]
    upstream = call(sum_four_body, shape(TOK, GROUP), moved=1 << 20)(place, *partials)
    upstream = send(upstream, TURN)

    query_grad, key_grad, value_grad = call(
        backward_body,
        (shape(TOK, GROUP), shape(TOK, HEAD), shape(TOK, HEAD)),
        flops=5 * 4 * 2 * TOK * TOK * HEAD,
        moved=3 << 20,
        limit=63,
    )(place, upstream, query_rows, key_rows, value_matrix, prob)

    pieces = call(sum_z_body, (shape(SHARD, GROUP),) * 2, moved=2 << 20)(place, grad_rows)
    pieces = [send(piece, pairs).astype(F32) for piece, pairs in zip(pieces, TO_OWNER)]
    weight_grad = pieces[0] + pieces[1]
    return (layer_out, query_grad, key_grad, value_grad, weight_grad.T)


def solution(mesh):
    placed = (
        P("dp", "mp"),
        P("dp", "mp"),
        P("dp", "mp"),
        P("mp", "dp"),
        P("dp", "mp"),
        P("dp", None),
    )
    return jax.shard_map(
        per_device,
        mesh=mesh,
        in_specs=placed,
        out_specs=(P("dp", "mp"), P("dp", "mp"), P("dp", "mp"), P("dp", "mp"), P("mp", "dp")),
        check_vma=False,
    )
```

```python
import jax
import jax.numpy as jnp
from jax import lax
from jax.experimental import pallas as pl
from jax.experimental.pallas import tpu as pltpu
from jax.sharding import PartitionSpec as P


NX, NZ, NC, NY = 4, 8, 2, 4
HEAD = 128
TOK = 256
HEADS = 4
GROUP = HEADS * HEAD
COLS = 1280
SHARD = 80
AXES = ("dp", "mp")
BF, F32 = jnp.bfloat16, jnp.float32
SCALE = HEAD ** -0.5


def route(target):
    pairs = []
    for x in range(NX):
        for z in range(NZ):
            for c in range(NC):
                for y in range(NY):
                    tx, tz, tc, ty = target(x, z, c, y)
                    src = ((x * NZ + z) * NC + c) * NY + y
                    pairs.append((src, ((tx * NZ + tz) * NC + tc) * NY + ty))
    return pairs


def low_of(x):
    return (x + x // 2) % 2


def chip(high, low):
    return 3 - low if high else low


SWAP = route(lambda x, z, c, y: (x, z, 1 - c, y))
ACROSS = route(lambda x, z, c, y: (x ^ 1, z, c, y))
OTHER = route(lambda x, z, c, y: (3 - x, z, c, y))
TO_PLANE = route(lambda x, z, c, y: (chip(c, y // 2), z, y % 2, x))
TO_OWNER = [
    route(lambda x, z, c, y, k=k: (y, z, (x // 2 + k) % 2, 2 * low_of(x) + c)) for k in range(2)
]
TURN = route(lambda x, z, c, y: (chip(x // 2, y // 2), z, y % 2, 2 * low_of(x) + c))
ALONG_Y = [route(lambda x, z, c, y, k=k: (x, z, c, (y + k) % 4)) for k in range(1, 4)]
Z_GROUPS = [[(x * NZ + z) * NC + c for z in range(NZ)] for x in range(NX) for c in range(NC)]


def send(value, pairs):
    return lax.ppermute(value, AXES, pairs)


def exchange(blocks, groups):
    return lax.all_to_all(blocks, "dp", 0, 0, axis_index_groups=groups, tiled=True)


def dot(a, b, dims):
    return lax.dot_general(a, b, (dims, ((), ())), preferred_element_type=F32)


def whole(array):
    dims = array.shape
    return pl.BlockSpec(dims, lambda i: (0,) * len(dims), pipeline_mode=pl.Buffered(1))


def place():
    dp = lax.axis_index("dp")
    x = dp // (NZ * NC)
    return 2 * low_of(x) + dp % NC, lax.axis_index("mp"), x // 2


def call(body, outs, scratch=(), flops=0, moved=0, limit=12, scalars=0):
    def run(*operands):
        return pl.pallas_call(
            body,
            out_shape=outs,
            grid=(1,),
            in_specs=[pl.BlockSpec(memory_space=pltpu.SMEM)] * scalars
            + [whole(a) for a in operands[scalars:]],
            out_specs=jax.tree.map(whole, outs),
            scratch_shapes=list(scratch),
            compiler_params=pltpu.CompilerParams(vmem_limit_bytes=limit << 20),
            cost_estimate=pl.CostEstimate(flops=flops, bytes_accessed=moved, transcendentals=0),
        )(*operands)

    return run


def shape(*dims, dtype=BF):
    return jax.ShapeDtypeStruct(dims, dtype)


def forward_body(lengths, q_ref, k_ref, v_ref, att_ref, prob_ref):
    rows = lax.broadcasted_iota(jnp.int32, (TOK, TOK), 0)
    cols = lax.broadcasted_iota(jnp.int32, (TOK, TOK), 1)
    row_at = lax.broadcasted_iota(jnp.int32, (TOK, 1), 0)
    col_at = lax.broadcasted_iota(jnp.int32, (1, TOK), 1)
    row_seg = jnp.zeros((TOK, 1), jnp.int32)
    col_seg = jnp.zeros((1, TOK), jnp.int32)
    end = jnp.int32(0)
    for i in range(8):
        end = end + lengths[i]
        row_seg = row_seg + (row_at >= end).astype(jnp.int32)
        col_seg = col_seg + (col_at >= end).astype(jnp.int32)
    allowed = (row_seg == col_seg) & (rows >= cols)
    for h in range(HEADS):
        at = slice(h * HEAD, (h + 1) * HEAD)
        logits = dot(q_ref[:, at], k_ref[...], ((1,), (1,))) * SCALE
        logits = jnp.where(allowed, logits, -jnp.inf)
        terms = jnp.exp(logits - jnp.max(logits, axis=-1, keepdims=True))
        prob = terms / jnp.sum(terms, axis=-1, keepdims=True)
        prob_ref[h] = prob
        att_ref[:, at] = dot(prob.astype(BF), v_ref[...], ((1,), (0,))).astype(BF)


def sum_four_body(a0, a1, a2, a3, out):
    out[...] = (
        (a0[...].astype(F32) + a1[...].astype(F32)) + (a2[...].astype(F32) + a3[...].astype(F32))
    ).astype(BF)


def backward_body(up_ref, q_ref, k_ref, v_ref, prob_ref, own, across, dq_ref, dk_ref, dv_ref, out):
    out[...] = (own[...].astype(F32) + across[...].astype(F32)).astype(BF)
    key_sum = jnp.zeros((TOK, HEAD), F32)
    value_sum = jnp.zeros((TOK, HEAD), F32)
    for h in range(HEADS):
        at = slice(h * HEAD, (h + 1) * HEAD)
        up = up_ref[:, at]
        prob = prob_ref[h]
        prob_grad = dot(up, v_ref[...], ((1,), (1,)))
        delta = jnp.sum(prob * prob_grad, axis=-1, keepdims=True)
        score = (prob * (prob_grad - delta) * SCALE).astype(BF)
        dq_ref[:, at] = dot(score, k_ref[...], ((1,), (0,))).astype(BF)
        key_sum = key_sum + dot(score, q_ref[:, at], ((0,), (0,)))
        value_sum = value_sum + dot(prob.astype(BF), up, ((0,), (0,)))
    dk_ref[...] = key_sum.astype(BF)
    dv_ref[...] = value_sum.astype(BF)


def weight_grad_body(o0, o1, o2, o3, r0, r1, r2, r3, grad_ref, att):
    g, y, _ = place()
    for k, ref in enumerate((r0, r1, r2, r3)):
        att[jnp.bitwise_xor((y + 4 - k) % 4, g)] = ref[...]
    for i in range(COLS // 256):
        at = slice(i * 256, (i + 1) * 256)
        total = dot(o0[:, at], att[0], ((0,), (0,)))
        for r, ref in ((1, o1), (2, o2), (3, o3)):
            total = total + dot(ref[:, at], att[r], ((0,), (0,)))
        grad_ref[at, :] = total.astype(BF)


def layer_pair_body(r0, r1, r2, r3, wt, pair_ref, att_ref, att):
    g, y, _ = place()
    for k, ref in enumerate((r0, r1, r2, r3)):
        att[jnp.bitwise_xor((y + 4 - k) % 4, g)] = ref[...]
    for i in range(2):
        pair_ref[i] = dot(att[2 * i + 1], wt[...], ((1,), (1,))).astype(BF)
        att_ref[i] = att[2 * i]


def layer_across_body(att, wt, pair, out):
    out[...] = (dot(att[1], wt[...], ((1,), (1,))) + pair[1].astype(F32)).astype(BF)


def layer_own_body(att, wt, pair, out):
    out[...] = (dot(att[0], wt[...], ((1,), (1,))) + pair[0].astype(F32)).astype(BF)


def attn_grad_body(o0, o1, o2, o3, w0, w1, g0, g1, g2, g3, wt_ref, og):
    g, y, high = place()
    for k, ref in enumerate((w0, w1)):
        c = (high + k) % 2
        for z in range(NZ):
            wt_ref[pl.ds(pl.multiple_of(z * 160 + c * SHARD, 16), SHARD), :] = ref[z]
    for r, ref in enumerate((o0, o1, o2, o3)):
        og[r] = ref[...]
    for k, ref in enumerate((g0, g1, g2, g3)):
        at = jnp.bitwise_xor((y + k) % 4, g)
        ref[...] = dot(og[at], wt_ref[...], ((1,), (0,))).astype(BF)


def sum_z_body(blocks, o0, o1):
    high = place()[2]
    for k, ref in enumerate((o0, o1)):
        at = pl.ds(pl.multiple_of((high + k) % 2 * SHARD, 16), SHARD)
        total = blocks[0, at, :].astype(F32)
        for z in range(1, NZ):
            total = total + blocks[z, at, :].astype(F32)
        ref[...] = total.astype(BF)


def per_device(query_rows, key_rows, value_matrix, out_weight, out_grad, doc_lengths):
    across_grad = send(out_grad, ACROSS)
    cols = [out_grad, send(out_grad, SWAP), across_grad, send(across_grad, SWAP)]

    wt = send(out_weight.T, TO_PLANE)
    wt = exchange(jnp.broadcast_to(wt[None], (NZ, SHARD, GROUP)), Z_GROUPS)
    blocks = [wt, send(wt, OTHER)]

    attended, prob = call(
        forward_body,
        (shape(TOK, GROUP), shape(HEADS, TOK, TOK, dtype=F32)),
        flops=4 * 4 * TOK * TOK * HEAD,
        moved=2 << 20,
        limit=63,
        scalars=1,
    )(doc_lengths[0], query_rows, key_rows, value_matrix)
    heads = send(attended, TURN)
    heads = [heads] + [send(heads, pairs) for pairs in ALONG_Y]

    big = 2 * 4 * TOK * COLS * GROUP
    grad_part = call(
        weight_grad_body,
        shape(COLS, GROUP),
        scratch=(pltpu.VMEM((4, TOK, GROUP), BF),),
        flops=big,
        moved=6 << 20,
    )(*cols, *heads)
    grad_rows = exchange(grad_part.reshape(NZ, 2 * SHARD, GROUP), Z_GROUPS)

    *partials, wt_all = call(
        attn_grad_body,
        (shape(TOK, GROUP),) * 4 + (shape(COLS, GROUP),),
        scratch=(pltpu.VMEM((4, TOK, COLS), BF),),
        flops=big,
        moved=6 << 20,
    )(*cols, *blocks)

    pair, attended_two = call(
        layer_pair_body,
        (shape(2, TOK, COLS), shape(2, TOK, GROUP)),
        scratch=(pltpu.VMEM((4, TOK, GROUP), BF),),
        flops=big // 2,
        moved=4 << 20,
    )(*heads, wt_all)
    pair = send(pair, SWAP)
    across = call(
        layer_across_body, shape(TOK, COLS), flops=big // 4, moved=3 << 20
    )(attended_two, wt_all, pair)
    across = send(across, ACROSS)
    own = call(layer_own_body, shape(TOK, COLS), flops=big // 4, moved=4 << 20)(
        attended_two, wt_all, pair
    )

    partials = [partials[0]] + [send(p, pairs) for p, pairs in zip(partials[1:], ALONG_Y)]
    upstream = call(sum_four_body, shape(TOK, GROUP), moved=1 << 20)(*partials)
    upstream = send(upstream, TURN)

    query_grad, key_grad, value_grad, layer_out = call(
        backward_body,
        (shape(TOK, GROUP), shape(TOK, HEAD), shape(TOK, HEAD), shape(TOK, COLS)),
        flops=5 * 4 * 2 * TOK * TOK * HEAD,
        moved=3 << 20,
        limit=63,
    )(upstream, query_rows, key_rows, value_matrix, prob, own, across)

    pieces = call(sum_z_body, (shape(SHARD, GROUP),) * 2, moved=2 << 20)(
        grad_rows
    )
    pieces = [send(piece, pairs).astype(F32) for piece, pairs in zip(pieces, TO_OWNER)]
    weight_grad = pieces[0] + pieces[1]
    return (layer_out, query_grad, key_grad, value_grad, weight_grad.T)


def solution(mesh):
    placed = (
        P("dp", "mp"),
        P("dp", "mp"),
        P("dp", "mp"),
        P("mp", "dp"),
        P("dp", "mp"),
        P("dp", None),
    )
    return jax.shard_map(
        per_device,
        mesh=mesh,
        in_specs=placed,
        out_specs=(P("dp", "mp"), P("dp", "mp"), P("dp", "mp"), P("dp", "mp"), P("mp", "dp")),
        check_vma=False,
    )
```

```python
import jax
import jax.numpy as jnp
from jax import lax
from jax.experimental import pallas as pl
from jax.experimental.pallas import tpu as pltpu
from jax.sharding import PartitionSpec as P


NX, NZ, NC, NY = 4, 8, 2, 4
HEAD = 128
TOK = 256
HEADS = 4
GROUP = HEADS * HEAD
COLS = 1280
SHARD = 80
AXES = ("dp", "mp")
BF, F32 = jnp.bfloat16, jnp.float32
SCALE = HEAD ** -0.5


def route(target):
    pairs = []
    for x in range(NX):
        for z in range(NZ):
            for c in range(NC):
                for y in range(NY):
                    tx, tz, tc, ty = target(x, z, c, y)
                    src = ((x * NZ + z) * NC + c) * NY + y
                    pairs.append((src, ((tx * NZ + tz) * NC + tc) * NY + ty))
    return pairs


def low_of(x):
    return (x + x // 2) % 2


def chip(high, low):
    return 3 - low if high else low


SWAP = route(lambda x, z, c, y: (x, z, 1 - c, y))
ACROSS = route(lambda x, z, c, y: (x ^ 1, z, c, y))
OTHER = route(lambda x, z, c, y: (3 - x, z, c, y))
TO_PLANE = route(lambda x, z, c, y: (chip(c, y // 2), z, y % 2, x))
TO_OWNER = [
    route(lambda x, z, c, y, k=k: (y, z, (x // 2 + k) % 2, 2 * low_of(x) + c)) for k in range(2)
]
TURN = route(lambda x, z, c, y: (chip(x // 2, y // 2), z, y % 2, 2 * low_of(x) + c))
ALONG_Y = [route(lambda x, z, c, y, k=k: (x, z, c, (y + k) % 4)) for k in range(1, 4)]
Z_GROUPS = [[(x * NZ + z) * NC + c for z in range(NZ)] for x in range(NX) for c in range(NC)]


def send(value, pairs):
    return lax.ppermute(value, AXES, pairs)


def exchange(blocks, groups):
    return lax.all_to_all(blocks, "dp", 0, 0, axis_index_groups=groups, tiled=True)


def dot(a, b, dims):
    return lax.dot_general(a, b, (dims, ((), ())), preferred_element_type=F32)


def whole(array):
    dims = array.shape
    return pl.BlockSpec(dims, lambda i: (0,) * len(dims), pipeline_mode=pl.Buffered(1))


def place():
    dp = lax.axis_index("dp")
    x = dp // (NZ * NC)
    return 2 * low_of(x) + dp % NC, lax.axis_index("mp"), x // 2


def call(body, outs, scratch=(), flops=0, moved=0, limit=12, scalars=0):
    def run(*operands):
        return pl.pallas_call(
            body,
            out_shape=outs,
            grid=(1,),
            in_specs=[pl.BlockSpec(memory_space=pltpu.SMEM)] * scalars
            + [whole(a) for a in operands[scalars:]],
            out_specs=jax.tree.map(whole, outs),
            scratch_shapes=list(scratch),
            compiler_params=pltpu.CompilerParams(vmem_limit_bytes=limit << 20),
            cost_estimate=pl.CostEstimate(flops=flops, bytes_accessed=moved, transcendentals=0),
        )(*operands)

    return run


def shape(*dims, dtype=BF):
    return jax.ShapeDtypeStruct(dims, dtype)


def forward_body(lengths, q_ref, k_ref, v_ref, att_ref, prob_ref, kept):
    kept[:, :GROUP] = q_ref[...]
    kept[:, GROUP : GROUP + HEAD] = k_ref[...]
    kept[:, GROUP + HEAD :] = v_ref[...]
    rows = lax.broadcasted_iota(jnp.int32, (TOK, TOK), 0)
    cols = lax.broadcasted_iota(jnp.int32, (TOK, TOK), 1)
    row_at = lax.broadcasted_iota(jnp.int32, (TOK, 1), 0)
    col_at = lax.broadcasted_iota(jnp.int32, (1, TOK), 1)
    row_seg = jnp.zeros((TOK, 1), jnp.int32)
    col_seg = jnp.zeros((1, TOK), jnp.int32)
    end = jnp.int32(0)
    for i in range(8):
        end = end + lengths[i]
        row_seg = row_seg + (row_at >= end).astype(jnp.int32)
        col_seg = col_seg + (col_at >= end).astype(jnp.int32)
    allowed = (row_seg == col_seg) & (rows >= cols)
    for h in range(HEADS):
        at = slice(h * HEAD, (h + 1) * HEAD)
        logits = dot(q_ref[:, at], k_ref[...], ((1,), (1,))) * SCALE
        logits = jnp.where(allowed, logits, -jnp.inf)
        terms = jnp.exp(logits - jnp.max(logits, axis=-1, keepdims=True))
        prob = terms / jnp.sum(terms, axis=-1, keepdims=True)
        prob_ref[h] = prob
        att_ref[:, at] = dot(prob.astype(BF), v_ref[...], ((1,), (0,))).astype(BF)


def sum_four_body(a0, a1, a2, a3, out):
    out[...] = (
        (a0[...].astype(F32) + a1[...].astype(F32)) + (a2[...].astype(F32) + a3[...].astype(F32))
    ).astype(BF)


def backward_body(up_ref, kept, prob_ref, own, across, dq_ref, dk_ref, dv_ref, out):
    out[...] = (own[...].astype(F32) + across[...].astype(F32)).astype(BF)
    keys, values = kept[:, GROUP : GROUP + HEAD], kept[:, GROUP + HEAD :]
    key_sum = jnp.zeros((TOK, HEAD), F32)
    value_sum = jnp.zeros((TOK, HEAD), F32)
    for h in range(HEADS):
        at = slice(h * HEAD, (h + 1) * HEAD)
        up = up_ref[:, at]
        prob = prob_ref[h]
        prob_grad = dot(up, values, ((1,), (1,)))
        delta = jnp.sum(prob * prob_grad, axis=-1, keepdims=True)
        score = (prob * (prob_grad - delta) * SCALE).astype(BF)
        dq_ref[:, at] = dot(score, keys, ((1,), (0,))).astype(BF)
        key_sum = key_sum + dot(score, kept[:, at], ((0,), (0,)))
        value_sum = value_sum + dot(prob.astype(BF), up, ((0,), (0,)))
    dk_ref[...] = key_sum.astype(BF)
    dv_ref[...] = value_sum.astype(BF)


def weight_grad_body(o0, o1, o2, o3, r0, r1, r2, r3, grad_ref, att):
    g, y, _ = place()
    for k, ref in enumerate((r0, r1, r2, r3)):
        att[jnp.bitwise_xor((y + 4 - k) % 4, g)] = ref[...]
    for i in range(COLS // 256):
        at = slice(i * 256, (i + 1) * 256)
        total = dot(o0[:, at], att[0], ((0,), (0,)))
        for r, ref in ((1, o1), (2, o2), (3, o3)):
            total = total + dot(ref[:, at], att[r], ((0,), (0,)))
        grad_ref[at, :] = total.astype(BF)


def layer_pair_body(r0, r1, r2, r3, w0, w1, pair_ref, att_ref, wt_ref, att):
    g, y, high = place()
    for k, ref in enumerate((r0, r1, r2, r3)):
        att[jnp.bitwise_xor((y + 4 - k) % 4, g)] = ref[...]
    for k, ref in enumerate((w0, w1)):
        c = (high + k) % 2
        for z in range(NZ):
            wt_ref[pl.ds(pl.multiple_of(z * 160 + c * SHARD, 16), SHARD), :] = ref[z]
    for i in range(2):
        pair_ref[i] = dot(att[2 * i + 1], wt_ref[...], ((1,), (1,))).astype(BF)
        att_ref[i] = att[2 * i]


def layer_across_body(att, wt, pair, out):
    out[...] = (dot(att[1], wt[...], ((1,), (1,))) + pair[1].astype(F32)).astype(BF)


def layer_own_body(att, wt, pair, out):
    out[...] = (dot(att[0], wt[...], ((1,), (1,))) + pair[0].astype(F32)).astype(BF)


def attn_grad_body(o0, o1, o2, o3, wt, g0, g1, g2, g3, og):
    g, y, _ = place()
    for r, ref in enumerate((o0, o1, o2, o3)):
        og[r] = ref[...]
    for k, ref in enumerate((g0, g1, g2, g3)):
        at = jnp.bitwise_xor((y + k) % 4, g)
        ref[...] = dot(og[at], wt[...], ((1,), (0,))).astype(BF)


def sum_z_body(blocks, o0, o1):
    high = place()[2]
    for k, ref in enumerate((o0, o1)):
        at = pl.ds(pl.multiple_of((high + k) % 2 * SHARD, 16), SHARD)
        total = blocks[0, at, :].astype(F32)
        for z in range(1, NZ):
            total = total + blocks[z, at, :].astype(F32)
        ref[...] = total.astype(BF)


def per_device(query_rows, key_rows, value_matrix, out_weight, out_grad, doc_lengths):
    across_grad = send(out_grad, ACROSS)
    cols = [out_grad, send(out_grad, SWAP), across_grad, send(across_grad, SWAP)]

    wt = send(out_weight.T, TO_PLANE)
    wt = exchange(jnp.broadcast_to(wt[None], (NZ, SHARD, GROUP)), Z_GROUPS)
    blocks = [wt, send(wt, OTHER)]

    attended, prob, kept = call(
        forward_body,
        (shape(TOK, GROUP), shape(HEADS, TOK, TOK, dtype=F32), shape(TOK, GROUP + 2 * HEAD)),
        flops=4 * 4 * TOK * TOK * HEAD,
        moved=2 << 20,
        limit=63,
        scalars=1,
    )(doc_lengths[0], query_rows, key_rows, value_matrix)
    heads = send(attended, TURN)
    heads = [heads] + [send(heads, pairs) for pairs in ALONG_Y]

    big = 2 * 4 * TOK * COLS * GROUP
    grad_part = call(
        weight_grad_body,
        shape(COLS, GROUP),
        scratch=(pltpu.VMEM((4, TOK, GROUP), BF),),
        flops=big,
        moved=6 << 20,
    )(*cols, *heads)
    grad_rows = exchange(grad_part.reshape(NZ, 2 * SHARD, GROUP), Z_GROUPS)

    pair, attended_two, wt_all = call(
        layer_pair_body,
        (shape(2, TOK, COLS), shape(2, TOK, GROUP), shape(COLS, GROUP)),
        scratch=(pltpu.VMEM((4, TOK, GROUP), BF),),
        flops=big // 2,
        moved=6 << 20,
    )(*heads, *blocks)
    partials = call(
        attn_grad_body,
        (shape(TOK, GROUP),) * 4,
        scratch=(pltpu.VMEM((4, TOK, COLS), BF),),
        flops=big,
        moved=6 << 20,
    )(*cols, wt_all)
    pair = send(pair, SWAP)
    across = call(
        layer_across_body, shape(TOK, COLS), flops=big // 4, moved=3 << 20
    )(attended_two, wt_all, pair)
    across = send(across, ACROSS)
    own = call(layer_own_body, shape(TOK, COLS), flops=big // 4, moved=4 << 20)(
        attended_two, wt_all, pair
    )

    partials = [partials[0]] + [send(p, pairs) for p, pairs in zip(partials[1:], ALONG_Y)]
    upstream = call(sum_four_body, shape(TOK, GROUP), moved=1 << 20)(*partials)
    upstream = send(upstream, TURN)

    query_grad, key_grad, value_grad, layer_out = call(
        backward_body,
        (shape(TOK, GROUP), shape(TOK, HEAD), shape(TOK, HEAD), shape(TOK, COLS)),
        flops=5 * 4 * 2 * TOK * TOK * HEAD,
        moved=3 << 20,
    )(upstream, kept, prob, own, across)

    pieces = call(sum_z_body, (shape(SHARD, GROUP),) * 2, moved=2 << 20)(
        grad_rows
    )
    pieces = [send(piece, pairs).astype(F32) for piece, pairs in zip(pieces, TO_OWNER)]
    weight_grad = pieces[0] + pieces[1]
    return (layer_out, query_grad, key_grad, value_grad, weight_grad.T)


def solution(mesh):
    placed = (
        P("dp", "mp"),
        P("dp", "mp"),
        P("dp", "mp"),
        P("mp", "dp"),
        P("dp", "mp"),
        P("dp", None),
    )
    return jax.shard_map(
        per_device,
        mesh=mesh,
        in_specs=placed,
        out_specs=(P("dp", "mp"), P("dp", "mp"), P("dp", "mp"), P("dp", "mp"), P("mp", "dp")),
        check_vma=False,
    )
```
